32 devices in a mesh: chan: 4 (over y, core), tile: 8 (over z, x).
Axes of the slice: x: 2, y: 2, z: 4, core: 2. Of those that a mesh axis runs over, the one named last changes fastest.
Arguments:
- dirty: float32 [2, 36, 128, 128], P(None, 'chan', 'tile'), may hold values from -6 to 6
- beams: float32 [36, 289], P('chan'), may hold values from -0.24 to 0.24
- chan_bins: int32 [36], replicated, may hold values from 0 to 287
- pixel_order: int32 [8, 2048], P('tile'), may hold values from 0 to 2047, each once within a row
Outputs:
- spectrum: float32 [2, 256, 8, 2048], P(None, None, 'tile', 'chan')
- residual: float32 [2, 36, 128, 128], P(None, 'chan', 'tile')
The draws below stay inside these ranges and needn't reach their ends.
Inputs may be any that keep to these rules, and one draw needn't show every extreme that they name: `pixel_order`: each row is a permutation of 0 to 2047.
All inputs are finite; a program needn't handle non-finite values.
Results may differ from the reference program's by a relative error of at most 0.000068.
Values sent between devices are 32-bit elements; how exact they have to be, the bound alone decides.
A program may use at most 64 MiB of HBM per device.

```python
import math
import jax
import jax.numpy as jnp
from jax import lax

CHANNELS = 36
DEPTHS = 256
BINS = 288
BEAM = 17
HALF = 8
NX = 128
NY = 128
TILES = 8
TILE_PIX = 2048


def with_ends(result, key, smallest, largest):
    spot = [jax.random.randint(jax.random.fold_in(key, axis), (), 0, length) for axis, length in enumerate(result.shape)]
    widest = result.shape.index(max(result.shape))
    next_to = spot[:widest] + [(spot[widest] + 1) % result.shape[widest]] + spot[widest + 1:]
    return result.at[tuple(spot)].set(smallest).at[tuple(next_to)].set(largest)


def block_levels(stream_key, dims, shards, low, high):
    loudness, own = 1.0, jax.random.fold_in(stream_key, 6)
    for dim, parts in shards:
        steps = jnp.exp(jax.random.uniform(jax.random.fold_in(own, dim), (parts,), jnp.float32, low / len(shards), high / len(shards)))
        loudness = loudness * jnp.repeat(steps, dims[dim] // parts).reshape([-1 if axis == dim else 1 for axis in range(len(dims))])
    return loudness


def centred(stream_key, extent, deviation, bound, cuts=(), kind=jnp.bfloat16):
    drawn = jax.random.normal(stream_key, extent, jnp.float32) * deviation
    if len(cuts) > 0:
        drawn = block_levels(stream_key, extent, cuts, -0.22, 0.18) * drawn
    return jnp.clip(drawn, min=-bound, max=bound).astype(kind)


def setup_inputs(seed: int = 0) -> dict:
    seeds = jax.random.split(jax.random.key(seed), 5)
    dirty = centred(seeds[0], (2, CHANNELS, NY, NX), 1.0, 6.0, ((1, 4), (2, 8)), jnp.float32)
    beams = centred(seeds[1], (CHANNELS, BEAM * BEAM), 0.04, 0.24, ((0, 4),), jnp.float32)
    chan_bins = with_ends(jax.random.randint(seeds[2], (CHANNELS,), 0, BINS), jax.random.fold_in(seeds[2], 1), 0, BINS - 1).astype(jnp.int32)
    pixel_order = jax.vmap(lambda own: jax.random.permutation(own, TILE_PIX))(jax.random.split(seeds[3], TILES)).reshape((TILES, TILE_PIX)).astype(jnp.int32)
    return {"dirty": dirty, "beams": beams, "chan_bins": chan_bins, "pixel_order": pixel_order}


THRESHOLD = 0.8
STEP_SIZE = 0.5
HIGH = lax.Precision.HIGHEST

def analysis_matrix(bin_list, channels):
    depth_index = jnp.arange(DEPTHS, dtype=jnp.int32) - DEPTHS // 2
    turn_count = jnp.mod(bin_list[:, None] * depth_index[None, :], BINS)
    angles = turn_count.astype(jnp.float32) * (2.0 * math.pi / BINS)
    cosine = jnp.cos(angles).T
    sine_part = jnp.sin(angles).T
    upper = jnp.concatenate([cosine, sine_part], axis=1)
    lower = jnp.concatenate([-sine_part, cosine], axis=1)
    return jnp.concatenate([upper, lower], axis=0) * (1.0 / math.sqrt(channels))

def shrink(spectra):
    depth_count = spectra.shape[0] // 2
    real_part = spectra[:depth_count]
    imag_part = spectra[depth_count:]
    magnitude = jnp.sqrt(real_part * real_part + imag_part * imag_part)
    factor = jnp.maximum(magnitude - THRESHOLD, 0.0) / jnp.maximum(magnitude, THRESHOLD)
    return spectra * jnp.concatenate([factor, factor], axis=0)

def blur(field, beams, row_pad):
    pair_count, chan_count, row_count, col_count = field.shape
    beam_width = math.isqrt(beams.shape[1])
    beam_edge = (beam_width - 1) // 2
    kernel = beams.reshape(chan_count, beam_width, beam_width)
    kernel = jnp.concatenate([kernel, kernel], axis=0)[:, None]
    stacked = field.reshape(1, pair_count * chan_count, row_count, col_count)
    blurred = lax.conv_general_dilated(stacked, kernel, (1, 1), ((row_pad, row_pad), (beam_edge, beam_edge)), feature_group_count=pair_count * chan_count, precision=HIGH)
    return blurred.reshape(pair_count, chan_count, blurred.shape[2], col_count)

def reference(dirty, beams, chan_bins, pixel_order):
    channels = chan_bins.shape[0]
    analysis = analysis_matrix(chan_bins, channels)
    observed = dirty.reshape(2 * channels, NY * NX)
    first = shrink(jnp.dot(analysis, observed, precision=HIGH, preferred_element_type=jnp.float32))
    model = jnp.dot(analysis.T, first, precision=HIGH, preferred_element_type=jnp.float32)
    model = model.reshape(2, channels, NY, NX)
    residual = dirty - blur(model, beams, HALF)
    update = jnp.dot(analysis, residual.reshape(2 * channels, NY * NX), precision=HIGH, preferred_element_type=jnp.float32)
    second = shrink(first + STEP_SIZE * update)
    arranged = second.reshape(2 * DEPTHS, TILES, TILE_PIX)
    slot_index = jnp.broadcast_to(pixel_order[None], arranged.shape)
    spectrum = jnp.take_along_axis(arranged, slot_index, axis=2).reshape(2, DEPTHS, TILES, TILE_PIX)
    return (spectrum, residual)
```

```python
import functools
import math

import jax
import jax.numpy as jnp
from jax import lax
from jax.experimental import pallas as pl
from jax.experimental.pallas import tpu as pltpu
from jax.sharding import PartitionSpec as P

DEPTHS = 256
BINS = 288
THRESHOLD = 0.8
STEP_SIZE = 0.5
MESH = pl.DeviceIdType.MESH
LANES = 128
REACH = 2
F32 = jnp.float32
BF16 = jnp.bfloat16


def round_up(value, unit):
    return (value + unit - 1) // unit * unit


def split(x):
    high = x.astype(BF16)
    return high, (x - high.astype(F32)).astype(BF16)


def shrink_pair(a, b):
    squared = a * a + b * b
    factor = jnp.maximum(1.0 - THRESHOLD * lax.rsqrt(jnp.maximum(squared, 1e-30)), 0.0)
    return a * factor, b * factor


def hops(half):
    last = -((REACH - half) // (REACH + 1))
    return [(REACH + 1) * m for m in range(-last, last + 1)]


def aligned(row):
    return row if isinstance(row, int) else pl.multiple_of(row, 8)


def mxu(a, b):
    return jnp.dot(a, b, preferred_element_type=F32)


def kernel(
    d,
    dirty_hbm,
    beams_hbm,
    bins_hbm,
    order_hbm,
    big,
    first_slots,
    res,
    dirty,
    beams,
    bins,
    order,
    wide,
    places,
    bands,
    bincol,
    at3,
    a3,
    at2,
    x,
    first_hi,
    first_lo,
    model,
    padded,
    slots,
    mixed,
    send_a,
    send_d,
    send_m,
    send_r,
    recv_a,
    recv_d,
    recv_m,
    recv_h,
    recv_r,
    sems_a,
    sems_d,
    sems_m,
    sems_h,
    sems_r,
    sems_in,
):
    G, T, R, Y, C, S, W, CC, NCH, HALF, BEAM = (
        d["G"], d["T"], d["R"], d["Y"], d["C"], d["S"], d["W"], d["CC"], d["NCH"], d["HALF"], d["BEAM"]
    )
    SC = S * C
    KP = d["KP"]
    g = lax.axis_index("chan")
    t = lax.axis_index("tile")
    has_prev = t > 0
    has_next = t < T - 1
    before = lax.rem(t + T - 1, T)
    after = lax.rem(t + 1, T)

    pairs = ((dirty_hbm, dirty), (bins_hbm, bins), (beams_hbm, beams), (order_hbm, order))
    loads = [pltpu.make_async_copy(src, dst, sems_in.at[n]) for n, (src, dst) in enumerate(pairs)]
    for load in loads:
        load.start()
    barrier = pltpu.get_barrier_semaphore()
    for step in range(1, G):
        pl.semaphore_signal(barrier, inc=1, device_id=(lax.rem(g + step, G), t), device_id_type=MESH)

    @pl.when(has_prev)
    def _():
        for p in range(G):
            pl.semaphore_signal(barrier, inc=1, device_id=(p, before), device_id_type=MESH)

    @pl.when(has_next)
    def _():
        for p in range(G):
            pl.semaphore_signal(barrier, inc=1, device_id=(p, after), device_id_type=MESH)

    def pack(send, k, cells):
        for p in range(G):
            for r in range(R):
                send[p, k, r * W : r * W + W, :] = cells[pl.ds(k * W * Y + p * R + r, W, stride=Y), :]

    loads[0].wait()
    for c in range(C):
        for s in range(S):
            mixed[(c * S + s) * Y : (c * S + s) * Y + Y, :] = dirty[(s * C + c) * Y : (s * C + c) * Y + Y, :]
    for k in range(NCH):
        pack(send_a, k, mixed)
    near = has_prev.astype(jnp.int32) + has_next.astype(jnp.int32)
    pl.semaphore_wait(barrier, G - 1 + G * near)

    def own_copies(src, dst, sems, *k):
        out_copies, in_copies = [], []
        for step in range(1, G):
            p = lax.rem(g + step, G)
            out_copies.append(
                pltpu.make_async_remote_copy(
                    src(p), dst(g), sems.at[(0, p, *k)], sems.at[(1, g, *k)], device_id=(p, t), device_id_type=MESH
                )
            )
            in_copies.append(
                pltpu.make_async_remote_copy(
                    src(p), dst(p), sems.at[(0, p, *k)], sems.at[(1, p, *k)], device_id=(p, t), device_id_type=MESH
                )
            )
        return out_copies, in_copies

    out_a, in_a = own_copies(lambda p: send_a.at[p], lambda p: recv_a.at[p], sems_a)
    for copy in out_a:
        copy.start()
    recv_a[g] = send_a[g]

    for load in loads[1:]:
        load.wait()
    bincol[...] = jnp.zeros_like(bincol)
    for row in range(G * C):
        bincol[S * row : S * row + S, :] = jnp.full((S, LANES), bins[row].astype(F32))
    scale = 1.0 / math.sqrt(G * C)
    at3[...] = jnp.zeros_like(at3)
    for piece in range(DEPTHS // LANES):
        shape = (KP, LANES)
        depth = lax.broadcasted_iota(jnp.int32, shape, 1) + (piece * LANES - DEPTHS // 2)
        product = bincol[...] * depth.astype(F32)
        turns = product - BINS * jnp.floor(product * (1.0 / BINS))
        turns = jnp.where(turns < 0, turns + BINS, turns)
        turns = jnp.where(turns >= BINS, turns - BINS, turns)
        angles = turns * (2.0 * math.pi / BINS)
        row = lax.broadcasted_iota(jnp.int32, shape, 0)
        is_q = (row & 1) == 0
        real = row < G * SC
        cosine = jnp.where(real, jnp.cos(angles) * scale, 0.0)
        sine = jnp.where(real, jnp.sin(angles) * scale, 0.0)
        for half, value in ((0, jnp.where(is_q, cosine, sine)), (1, jnp.where(is_q, -sine, cosine))):
            lanes = pl.ds(half * DEPTHS + piece * LANES, LANES)
            high, low = split(value)
            at2[0:KP, lanes] = high
            at2[KP : 2 * KP, lanes] = low
            at3[0:KP, lanes] = high.astype(F32)
            at3[KP : 2 * KP, lanes] = low.astype(F32)
            at3[2 * KP : 3 * KP, lanes] = high.astype(F32)
    a3[...] = at3[...].T.astype(BF16)
    x[...] = jnp.zeros_like(x)

    shift = int(math.log2(LANES))
    PY = Y + 2 * HALF
    groups = hops(HALF)
    GY = len(groups) * Y
    near_lanes = list(range(-REACH, REACH + 1))
    per = LANES // PY
    wide[...] = jnp.zeros_like(wide)
    CP = round_up(C, 8)
    chunks = wide.shape[0] // CP
    for m in range(chunks):
        size = min(LANES, BEAM * BEAM - m * LANES)
        wide[m * CP : m * CP + C, 0:size] = beams[:, m * LANES : m * LANES + size]
    lane8 = lax.broadcasted_iota(jnp.int32, (8, LANES), 1)
    line8 = lax.broadcasted_iota(jnp.int32, (8, LANES), 0)
    for n, turn in enumerate(groups):
        low = -REACH if turn <= 0 else 0
        high = REACH if turn >= 0 else 0
        for y in range(0, Y, 8):
            i = lax.rem(lane8, PY) - (line8 + y)
            for block in range(2):
                j0 = lane8 // PY - REACH if block == 0 else jnp.where(lane8 < 2 * PY, REACH, LANES)
                j = j0 + (HALF + turn)
                ok = (i >= 0) & (i < BEAM) & (j0 >= low) & (j0 <= high) & (j >= 0) & (j < BEAM)
                places[pl.ds((block * len(groups) + n) * Y + y, 8), :] = jnp.where(ok, i * BEAM + j, -1)

    def band(c, carry):
        rows = [
            jnp.broadcast_to(wide[pl.ds(m * CP + c, 1), :], (8, LANES)) for m in range(chunks)
        ]
        for n, turn in enumerate(groups):
            parts = []
            for block in range(2):
                if block == 1 and turn < 0:
                    parts.append((jnp.zeros((Y, LANES), BF16),) * 2)
                    continue
                halves = []
                for y in range(0, Y, 8):
                    place = places[pl.ds((block * len(groups) + n) * Y + y, 8), :]
                    col = place & (LANES - 1)
                    row = lax.shift_right_arithmetic(place, shift)
                    acc = jnp.zeros((8, LANES), F32)
                    for m, source in enumerate(rows):
                        taken = jnp.take_along_axis(source, col, axis=1, mode="promise_in_bounds")
                        acc = jnp.where(row == m, taken, acc)
                    halves.append(acc)
                parts.append(split(jnp.concatenate(halves, axis=0)))
            for h in range(2):
                target = pl.ds(pl.multiple_of(c * (2 * GY) + h * GY + n * Y, 16), Y)
                bands[target, 0:LANES] = parts[0][h]
                bands[target, LANES : 2 * LANES] = parts[0][h]
                bands[target, 2 * LANES : 3 * LANES] = parts[1][h]
        return carry

    lax.fori_loop(0, C, band, 0)

    def permute(cells):
        halves = []
        for h in range(Y // 8):
            pixel = order[8 * h : 8 * h + 8, :]
            col = pixel & (LANES - 1)
            row = lax.shift_right_logical(pixel, shift)
            acc = jnp.zeros((8, LANES), F32)
            for y in range(Y):
                taken = jnp.take_along_axis(cells(y), col, axis=1, mode="promise_in_bounds")
                acc = jnp.where(row == y, taken, acc)
            halves.append(acc)
        return jnp.concatenate(halves, axis=0)

    def gather_dirty(c, carry):
        for s in range(S):
            source = (s * C + c) * Y
            target = pl.ds(aligned((c * S + s) * Y), Y)
            slots[target, :] = permute(lambda y: jnp.broadcast_to(dirty[pl.ds(source + y, 1), :], (8, LANES)))
        return carry

    def project(recv):
        for q in range(G):
            for k in range(NCH):
                for r in range(R):
                    x[q * SC + k * W : q * SC + k * W + W, r * LANES : (r + 1) * LANES] = recv[
                        q, k, r * W : r * W + W, :
                    ]
        high, low = split(x[...])
        parts = [high, high, low]
        if d["K3"] > 3 * KP:
            parts.append(jnp.zeros((d["K3"] - 3 * KP, x.shape[1]), BF16))
        big[...] = mxu(a3[...], jnp.concatenate(parts, axis=0))

    BLOCK = 16

    for copy in in_a:
        copy.wait_recv()
    project(recv_a)

    def shrink_first(i, carry):
        top = pl.ds(pl.multiple_of(i * BLOCK, BLOCK), BLOCK)
        low = pl.ds(pl.multiple_of(DEPTHS + i * BLOCK, BLOCK), BLOCK)
        a, b = shrink_pair(big[top, :], big[low, :])
        first_hi[top, :], first_lo[top, :] = split(a)
        first_hi[low, :], first_lo[low, :] = split(b)
        return carry

    lax.fori_loop(0, DEPTHS // BLOCK, shrink_first, 0)
    both = mxu(at2[...], first_hi[...])
    model[...] = both[:KP] + both[KP:] + mxu(at2[0:KP, :], first_lo[...])

    up = g * R < HALF
    goes = jnp.logical_or(jnp.logical_and(up, has_prev), jnp.logical_and(jnp.logical_not(up), has_next))
    toward = jnp.where(up, before, after)
    copies_m, copies_h = [], []
    for k in range(NCH):
        for p in range(G):
            for r in range(R):
                send_m[p, k, r * W : r * W + W, :] = model[
                    p * SC + k * W : p * SC + k * W + W, r * LANES : (r + 1) * LANES
                ]
        halo = [
            pltpu.make_async_remote_copy(
                send_m.at[p, k],
                recv_h.at[g, k],
                sems_h.at[0, p, k],
                sems_h.at[1, g, k],
                device_id=(p, toward),
                device_id_type=MESH,
            )
            for p in range(G)
        ]
        copies_h.append(halo)

        @pl.when(goes)
        def _():
            for copy in halo:
                copy.start()

        copies = own_copies(
            lambda p: send_m.at[p, k], lambda p: recv_m.at[p, k], sems_m, k
        )
        copies_m.append(copies)
        for copy in copies[0]:
            copy.start()
        recv_m[g, k] = send_m[g, k]

    lax.fori_loop(0, C, gather_dirty, 0)
    for k in range(NCH):
        pack(send_d, k, slots)
    out_d, in_d = own_copies(lambda p: send_d.at[p], lambda p: recv_d.at[p], sems_d)
    for copy in out_d:
        copy.start()
    recv_d[g] = send_d[g]

    lane = lax.broadcasted_iota(jnp.int32, (PY, LANES), 1)

    def moved(rows, by):
        if by == 0:
            return rows
        at = lane[: rows.shape[0]] + by
        return jnp.where((at >= 0) & (at < LANES), pltpu.roll(rows, (-by) % LANES, axis=1), 0.0)

    def convolve(c):
        images = [padded[pl.ds((c * S + s) * PY, PY), :] for s in range(S)]
        high, low = [], []
        for by in near_lanes:
            pairs = [split(moved(image, by)) for image in images]
            high.append(jnp.concatenate([pair[0] for pair in pairs], axis=1))
            low.append(jnp.concatenate([pair[1] for pair in pairs], axis=1))
        rest = jnp.zeros((LANES - 2 * PY, S * LANES), BF16)
        right = jnp.concatenate(high[:per] + low[:per] + high[per:] + low[per:] + [rest], axis=0)
        sums = mxu(bands[c * 2 * GY : (c + 1) * 2 * GY, :], right)
        for s in range(S):
            total = None
            for n, turn in enumerate(groups):
                span, lanes = slice(n * Y, (n + 1) * Y), slice(s * LANES, (s + 1) * LANES)
                term = moved(sums[span, lanes] + sums[GY + n * Y : GY + (n + 1) * Y, lanes], turn)
                total = term if total is None else total + term
            cells = pl.ds((s * C + c) * Y, Y)
            res[cells, :] = dirty[cells, :] - total

    def gather_res(c, carry):
        for s in range(S):
            source = (s * C + c) * Y
            target = pl.ds(aligned((c * S + s) * Y), Y)
            slots[target, :] = permute(lambda y: jnp.broadcast_to(res[pl.ds(source + y, 1), :], (8, LANES)))
        return carry

    def halo_block(q, k, ok):
        arrived = pltpu.make_async_remote_copy(
            send_m.at[q, k],
            recv_h.at[q, k],
            sems_h.at[0, q, k],
            sems_h.at[1, q, k],
            device_id=(q, t),
            device_id_type=MESH,
        )

        @pl.when(ok)
        def _():
            arrived.wait_recv()

        @pl.when(jnp.logical_not(ok))
        def _():
            recv_h[q, k] = jnp.zeros(recv_h.shape[2:], F32)

    copies_r = []

    def send_slots(k):
        pack(send_r, k, slots)
        copies = own_copies(lambda p: send_r.at[p, k], lambda p: recv_r.at[p, k], sems_r, k)
        copies_r.append(copies)
        for copy in copies[0]:
            copy.start()
        recv_r[g, k] = send_r[g, k]

    for k in range(NCH):
        for copy in copies_m[k][1]:
            copy.wait_recv()
        for q in range(G):
            from_next = q * R < HALF
            halo_block(q, k, has_next if from_next else has_prev)
            at_row = Y + HALF + q * R if from_next else q * R - HALF
            for r in range(R):
                padded[pl.ds(k * W * PY + HALF + q * R + r, W, stride=PY), :] = recv_m[
                    q, k, r * W : r * W + W, :
                ]
                padded[pl.ds(k * W * PY + at_row + r, W, stride=PY), :] = recv_h[
                    q, k, r * W : r * W + W, :
                ]
        for c in range(k * CC, (k + 1) * CC):
            convolve(c)
        for c in range(k * CC, (k + 1) * CC):
            gather_res(c, 0)
        send_slots(k)

    for copy in in_d:
        copy.wait_recv()
    project(recv_d)

    def shrink_slots(i, carry):
        top = pl.ds(pl.multiple_of(i * BLOCK, BLOCK), BLOCK)
        low = pl.ds(pl.multiple_of(DEPTHS + i * BLOCK, BLOCK), BLOCK)
        first_slots[top, :], first_slots[low, :] = shrink_pair(big[top, :], big[low, :])
        return carry

    lax.fori_loop(0, DEPTHS // BLOCK, shrink_slots, 0)

    for k in range(NCH):
        for copy in copies_r[k][1]:
            copy.wait_recv()
    project(recv_r)

    for copy in out_a + out_d:
        copy.wait_send()
    for k in range(NCH):
        for copy in copies_m[k][0] + copies_r[k][0]:
            copy.wait_send()

    @pl.when(goes)
    def _():
        for halo in copies_h:
            for copy in halo:
                copy.wait_send()


PARTS = 4


def finish_kernel(R, update, first, cells, out, res, stage, sems):
    copies = [pltpu.make_async_copy(cells, res, sems.at[0])]
    copies[0].start()
    block = 16

    def shrink_second(i, carry):
        top = pl.ds(pl.multiple_of(i * block, block), block)
        low = pl.ds(pl.multiple_of(DEPTHS + i * block, block), block)
        a, b = shrink_pair(
            first[top, :] + STEP_SIZE * update[top, :], first[low, :] + STEP_SIZE * update[low, :]
        )
        for start, value in ((0, a), (DEPTHS, b)):
            for r in range(R):
                stage[pl.ds((start + i * block) * R + r, block, stride=R), :] = value[
                    :, r * LANES : (r + 1) * LANES
                ]
        return carry

    steps = DEPTHS // block // PARTS
    rows = DEPTHS * R // PARTS
    for part in range(PARTS):
        lax.fori_loop(part * steps, (part + 1) * steps, shrink_second, 0)
        for half in range(2):
            span = pl.ds(half * DEPTHS * R + part * rows, rows)
            copy = pltpu.make_async_copy(stage.at[span], out.at[span], sems.at[1 + 2 * part + half])
            copy.start()
            copies.append(copy)
    for copy in copies:
        copy.wait()


def on_device(dirty, beams, chan_bins, pixel_order):
    S, C, Y, X = dirty.shape
    G = lax.axis_size("chan")
    T = lax.axis_size("tile")
    BEAM = math.isqrt(beams.shape[1])
    HALF = (BEAM - 1) // 2
    R = Y // G
    CC = 3 if C % 3 == 0 else C
    NCH = C // CC
    W = S * CC
    SC = S * C
    KP = round_up(G * SC, 16)
    K3 = round_up(3 * KP, LANES)
    PB = round_up(R * W, 8)
    N = R * X
    d = dict(G=G, T=T, R=R, Y=Y, C=C, S=S, W=W, CC=CC, NCH=NCH, HALF=HALF, BEAM=BEAM, KP=KP, K3=K3)
    vmem = pl.BlockSpec(memory_space=pltpu.VMEM)
    hbm = pl.BlockSpec(memory_space=pltpu.HBM)
    block = pltpu.VMEM((G, NCH, PB, LANES), F32)
    dma = pltpu.SemaphoreType.DMA
    args = (dirty.reshape(SC * Y, X), beams, chan_bins, pixel_order.reshape(Y, X))
    update, first, cells = pl.pallas_call(
        functools.partial(kernel, d),
        out_shape=(
            jax.ShapeDtypeStruct((2 * DEPTHS, N), F32),
            jax.ShapeDtypeStruct((2 * DEPTHS, N), F32),
            jax.ShapeDtypeStruct((SC * Y, X), F32),
        ),
        in_specs=[hbm, hbm, hbm, hbm],
        out_specs=(vmem, vmem, vmem),
        scratch_shapes=[
            pltpu.VMEM((SC * Y, X), F32),
            pltpu.VMEM(beams.shape, F32),
            pltpu.SMEM(chan_bins.shape, jnp.int32),
            pltpu.VMEM((Y, X), jnp.int32),
            pltpu.VMEM((pl.cdiv(beams.shape[1], LANES) * round_up(C, 8), LANES), F32),
            pltpu.VMEM((2 * len(hops(HALF)) * Y, LANES), jnp.int32),
            pltpu.VMEM((C * 2 * len(hops(HALF)) * Y, 3 * LANES), BF16),
            pltpu.VMEM((KP, LANES), F32),
            pltpu.VMEM((K3, 2 * DEPTHS), F32),
            pltpu.VMEM((2 * DEPTHS, K3), BF16),
            pltpu.VMEM((2 * KP, 2 * DEPTHS), BF16),
            pltpu.VMEM((KP, N), F32),
            pltpu.VMEM((2 * DEPTHS, N), BF16),
            pltpu.VMEM((2 * DEPTHS, N), BF16),
            pltpu.VMEM((KP, N), F32),
            pltpu.VMEM(((SC + 1) * (Y + 2 * HALF), LANES), F32),
            pltpu.VMEM(((SC + 1) * Y, LANES), F32),
            pltpu.VMEM(((SC + 1) * Y, LANES), F32),
        ]
        + [block] * 9
        + [dma((2, G)), dma((2, G)), dma((2, G, NCH)), dma((2, G, NCH)), dma((2, G, NCH)), dma((4,))],
        compiler_params=pltpu.CompilerParams(
            collective_id=0, has_side_effects=True, vmem_limit_bytes=40 * 1024 * 1024
        ),
    )(*(pltpu.with_memory_space_constraint(arg, pltpu.HBM) for arg in args))
    spectrum, residual = pl.pallas_call(
        functools.partial(finish_kernel, R),
        out_shape=(
            jax.ShapeDtypeStruct((2 * DEPTHS * R, LANES), F32),
            jax.ShapeDtypeStruct((SC * Y, X), F32),
        ),
        in_specs=[vmem, vmem, vmem],
        out_specs=(hbm, hbm),
        scratch_shapes=[pltpu.VMEM((2 * DEPTHS * R + 8, LANES), F32), dma((1 + 2 * PARTS,))],
        compiler_params=pltpu.CompilerParams(vmem_limit_bytes=8 * 1024 * 1024),
    )(update, first, cells)
    return spectrum.reshape(2, DEPTHS, 1, N), residual.reshape(dirty.shape)


def solution(mesh):
    placed = (P(None, "chan", "tile", None), P("chan", None), P(), P("tile", None))
    return jax.shard_map(
        on_device,
        mesh=mesh,
        in_specs=placed,
        out_specs=(P(None, None, "tile", "chan"), P(None, "chan", "tile", None)),
        check_vma=False,
    )
```

```python
import functools
import math

import jax
import jax.numpy as jnp
from jax import lax
from jax.experimental import pallas as pl
from jax.experimental.pallas import tpu as pltpu
from jax.sharding import PartitionSpec as P

DEPTHS = 256
BINS = 288
THRESHOLD = 0.8
STEP_SIZE = 0.5
MESH = pl.DeviceIdType.MESH
LANES = 128
REACH = 2
F32 = jnp.float32
BF16 = jnp.bfloat16


def round_up(value, unit):
    return (value + unit - 1) // unit * unit


def split(x):
    high = x.astype(BF16)
    return high, (x - high.astype(F32)).astype(BF16)


def shrink_pair(a, b):
    squared = a * a + b * b
    factor = jnp.maximum(1.0 - THRESHOLD * lax.rsqrt(jnp.maximum(squared, 1e-30)), 0.0)
    return a * factor, b * factor


def hops(half):
    last = -((REACH - half) // (REACH + 1))
    return [(REACH + 1) * m for m in range(-last, last + 1)]


def aligned(row):
    return row if isinstance(row, int) else pl.multiple_of(row, 8)


def mxu(a, b):
    return jnp.dot(a, b, preferred_element_type=F32)


def kernel(
    d,
    dirty_hbm,
    beams_hbm,
    bins_hbm,
    order_hbm,
    big,
    first_slots,
    res,
    dirty,
    beams,
    bins,
    order,
    wide,
    places,
    bands,
    bincol,
    at3,
    a3,
    at2,
    x,
    first_hi,
    first_lo,
    model,
    padded,
    slots,
    mixed,
    send_a,
    send_d,
    send_m,
    send_r,
    recv_a,
    recv_d,
    recv_m,
    recv_h,
    recv_r,
    sent,
    got_a,
    got_d,
    got_m,
    got_h,
    got_r,
    sems_in,
    joined,
):
    G, T, R, Y, C, S, W, CC, NCH, HALF, BEAM = (
        d["G"], d["T"], d["R"], d["Y"], d["C"], d["S"], d["W"], d["CC"], d["NCH"], d["HALF"], d["BEAM"]
    )
    SC = S * C
    KP = d["KP"]
    g = lax.axis_index("chan")
    t = lax.axis_index("tile")
    has_prev = t > 0
    has_next = t < T - 1
    before = lax.rem(t + T - 1, T)
    after = lax.rem(t + 1, T)

    pairs = ((dirty_hbm, dirty), (bins_hbm, bins), (beams_hbm, beams), (order_hbm, order))
    loads = [pltpu.make_async_copy(src, dst, sems_in.at[n]) for n, (src, dst) in enumerate(pairs)]
    for load in loads:
        load.start()
    last, lead = G - 1, G - 2
    barrier = pltpu.get_barrier_semaphore()
    for p in range(last):

        @pl.when(g != p)
        def _():
            pl.semaphore_signal(barrier, inc=1, device_id=(p, t), device_id_type=MESH)

    def pack(send, k, cells):
        for p in range(G):
            for r in range(R):
                send[p, k, r * W : r * W + W, :] = cells[pl.ds(k * W * Y + p * R + r, W, stride=Y), :]

    loads[0].wait()
    for c in range(C):
        for s in range(S):
            mixed[(c * S + s) * Y : (c * S + s) * Y + Y, :] = dirty[(s * C + c) * Y : (s * C + c) * Y + Y, :]
    for k in range(NCH):
        pack(send_a, k, mixed)
    @pl.when(g != last)
    def _():
        pl.semaphore_wait(barrier, G - 1)

    @pl.when(g == lead)
    def _():
        pl.semaphore_signal(joined, inc=1, device_id=(last, t), device_id_type=MESH)

        @pl.when(has_prev)
        def _():
            pl.semaphore_signal(barrier, inc=1, device_id=(last, before), device_id_type=MESH)

        @pl.when(has_next)
        def _():
            pl.semaphore_signal(barrier, inc=1, device_id=(last, after), device_id_type=MESH)

    @pl.when(g == last)
    def _():
        pl.semaphore_wait(joined, 1)

    def own_copies(src, dst, kind, got):
        copies = []
        for step in range(1, G):
            p = lax.rem(g + step, G)
            copies.append(
                pltpu.make_async_remote_copy(
                    src(p), dst(g), sent.at[kind], got, device_id=(p, t), device_id_type=MESH
                )
            )
        return copies

    def await_bytes(ref, sem):
        pltpu.make_async_copy(ref, ref, sem).wait()

    out_a = own_copies(lambda p: send_a.at[p], lambda p: recv_a.at[p], 0, got_a.at[0])
    for copy in out_a:
        copy.start()
    recv_a[g] = send_a[g]

    for load in loads[1:]:
        load.wait()
    bincol[...] = jnp.zeros_like(bincol)
    for row in range(G * C):
        bincol[S * row : S * row + S, :] = jnp.full((S, LANES), bins[row].astype(F32))
    scale = 1.0 / math.sqrt(G * C)
    at3[...] = jnp.zeros_like(at3)
    for piece in range(DEPTHS // LANES):
        shape = (KP, LANES)
        depth = lax.broadcasted_iota(jnp.int32, shape, 1) + (piece * LANES - DEPTHS // 2)
        product = bincol[...] * depth.astype(F32)
        turns = product - BINS * jnp.floor(product * (1.0 / BINS))
        turns = jnp.where(turns < 0, turns + BINS, turns)
        turns = jnp.where(turns >= BINS, turns - BINS, turns)
        angles = turns * (2.0 * math.pi / BINS)
        row = lax.broadcasted_iota(jnp.int32, shape, 0)
        is_q = (row & 1) == 0
        real = row < G * SC
        cosine = jnp.where(real, jnp.cos(angles) * scale, 0.0)
        sine = jnp.where(real, jnp.sin(angles) * scale, 0.0)
        for half, value in ((0, jnp.where(is_q, cosine, sine)), (1, jnp.where(is_q, -sine, cosine))):
            lanes = pl.ds(half * DEPTHS + piece * LANES, LANES)
            high, low = split(value)
            at2[0:KP, lanes] = high
            at2[KP : 2 * KP, lanes] = low
            at3[0:KP, lanes] = high.astype(F32)
            at3[KP : 2 * KP, lanes] = low.astype(F32)
            at3[2 * KP : 3 * KP, lanes] = high.astype(F32)
    a3[...] = at3[...].T.astype(BF16)
    x[...] = jnp.zeros_like(x)

    shift = int(math.log2(LANES))
    PY = Y + 2 * HALF
    groups = hops(HALF)
    GY = len(groups) * Y
    near_lanes = list(range(-REACH, REACH + 1))
    per = LANES // PY
    wide[...] = jnp.zeros_like(wide)
    CP = round_up(C, 8)
    chunks = wide.shape[0] // CP
    for m in range(chunks):
        size = min(LANES, BEAM * BEAM - m * LANES)
        wide[m * CP : m * CP + C, 0:size] = beams[:, m * LANES : m * LANES + size]
    lane8 = lax.broadcasted_iota(jnp.int32, (8, LANES), 1)
    line8 = lax.broadcasted_iota(jnp.int32, (8, LANES), 0)
    for n, turn in enumerate(groups):
        low = -REACH if turn <= 0 else 0
        high = REACH if turn >= 0 else 0
        for y in range(0, Y, 8):
            i = lax.rem(lane8, PY) - (line8 + y)
            for block in range(2):
                j0 = lane8 // PY - REACH if block == 0 else jnp.where(lane8 < 2 * PY, REACH, LANES)
                j = j0 + (HALF + turn)
                ok = (i >= 0) & (i < BEAM) & (j0 >= low) & (j0 <= high) & (j >= 0) & (j < BEAM)
                places[pl.ds((block * len(groups) + n) * Y + y, 8), :] = jnp.where(ok, i * BEAM + j, -1)

    def band(c, carry):
        rows = [
            jnp.broadcast_to(wide[pl.ds(m * CP + c, 1), :], (8, LANES)) for m in range(chunks)
        ]
        for n, turn in enumerate(groups):
            parts = []
            for block in range(2):
                if block == 1 and turn < 0:
                    parts.append((jnp.zeros((Y, LANES), BF16),) * 2)
                    continue
                halves = []
                for y in range(0, Y, 8):
                    place = places[pl.ds((block * len(groups) + n) * Y + y, 8), :]
                    col = place & (LANES - 1)
                    row = lax.shift_right_arithmetic(place, shift)
                    acc = jnp.zeros((8, LANES), F32)
                    for m, source in enumerate(rows):
                        taken = jnp.take_along_axis(source, col, axis=1, mode="promise_in_bounds")
                        acc = jnp.where(row == m, taken, acc)
                    halves.append(acc)
                parts.append(split(jnp.concatenate(halves, axis=0)))
            for h in range(2):
                target = pl.ds(pl.multiple_of(c * (2 * GY) + h * GY + n * Y, 16), Y)
                bands[target, 0:LANES] = parts[0][h]
                bands[target, LANES : 2 * LANES] = parts[0][h]
                bands[target, 2 * LANES : 3 * LANES] = parts[1][h]
        return carry

    lax.fori_loop(0, C, band, 0)

    def permute(cells):
        halves = []
        for h in range(Y // 8):
            pixel = order[8 * h : 8 * h + 8, :]
            col = pixel & (LANES - 1)
            row = lax.shift_right_logical(pixel, shift)
            acc = jnp.zeros((8, LANES), F32)
            for y in range(Y):
                taken = jnp.take_along_axis(cells(y), col, axis=1, mode="promise_in_bounds")
                acc = jnp.where(row == y, taken, acc)
            halves.append(acc)
        return jnp.concatenate(halves, axis=0)

    def gather_dirty(c, carry):
        for s in range(S):
            source = (s * C + c) * Y
            target = pl.ds(aligned((c * S + s) * Y), Y)
            slots[target, :] = permute(lambda y: jnp.broadcast_to(dirty[pl.ds(source + y, 1), :], (8, LANES)))
        return carry

    def project(recv):
        for q in range(G):
            for k in range(NCH):
                for r in range(R):
                    x[q * SC + k * W : q * SC + k * W + W, r * LANES : (r + 1) * LANES] = recv[
                        q, k, r * W : r * W + W, :
                    ]
        high, low = split(x[...])
        parts = [high, high, low]
        if d["K3"] > 3 * KP:
            parts.append(jnp.zeros((d["K3"] - 3 * KP, x.shape[1]), BF16))
        big[...] = mxu(a3[...], jnp.concatenate(parts, axis=0))

    BLOCK = 16

    @pl.when(g == last)
    def _():
        pl.semaphore_wait(barrier, has_prev.astype(jnp.int32) + has_next.astype(jnp.int32))
        for p in range(last):
            pl.semaphore_signal(joined, inc=1, device_id=(p, t), device_id_type=MESH)

    await_bytes(recv_a.at[0:last], got_a.at[0])
    project(recv_a)

    def shrink_first(i, carry):
        top = pl.ds(pl.multiple_of(i * BLOCK, BLOCK), BLOCK)
        low = pl.ds(pl.multiple_of(DEPTHS + i * BLOCK, BLOCK), BLOCK)
        a, b = shrink_pair(big[top, :], big[low, :])
        first_hi[top, :], first_lo[top, :] = split(a)
        first_hi[low, :], first_lo[low, :] = split(b)
        return carry

    lax.fori_loop(0, DEPTHS // BLOCK, shrink_first, 0)
    both = mxu(at2[...], first_hi[...])
    model[...] = both[:KP] + both[KP:] + mxu(at2[0:KP, :], first_lo[...])

    up = g * R < HALF
    goes = jnp.logical_or(jnp.logical_and(up, has_prev), jnp.logical_and(jnp.logical_not(up), has_next))
    toward = jnp.where(up, before, after)
    copies_h = []

    @pl.when(g != last)
    def _():
        pl.semaphore_wait(joined, 1)

    for k in range(NCH):
        for p in range(G):
            for r in range(R):
                send_m[p, k, r * W : r * W + W, :] = model[
                    p * SC + k * W : p * SC + k * W + W, r * LANES : (r + 1) * LANES
                ]
        halo = [
            pltpu.make_async_remote_copy(
                send_m.at[p, k],
                recv_h.at[g, k],
                sent.at[4],
                got_h.at[up.astype(jnp.int32), k],
                device_id=(p, toward),
                device_id_type=MESH,
            )
            for p in range(G)
        ]
        copies_h.append(halo)

        @pl.when(goes)
        def _():
            for copy in halo:
                copy.start()

        for copy in own_copies(lambda p: send_m.at[p, k], lambda p: recv_m.at[p, k], 2, got_m.at[k]):
            copy.start()
        recv_m[g, k] = send_m[g, k]

    lax.fori_loop(0, C, gather_dirty, 0)
    for k in range(NCH):
        pack(send_d, k, slots)
    for copy in own_copies(lambda p: send_d.at[p], lambda p: recv_d.at[p], 1, got_d.at[0]):
        copy.start()
    recv_d[g] = send_d[g]

    lane = lax.broadcasted_iota(jnp.int32, (PY, LANES), 1)

    def moved(rows, by):
        if by == 0:
            return rows
        at = lane[: rows.shape[0]] + by
        return jnp.where((at >= 0) & (at < LANES), pltpu.roll(rows, (-by) % LANES, axis=1), 0.0)

    def convolve(c):
        images = [padded[pl.ds((c * S + s) * PY, PY), :] for s in range(S)]
        high, low = [], []
        for by in near_lanes:
            pairs = [split(moved(image, by)) for image in images]
            high.append(jnp.concatenate([pair[0] for pair in pairs], axis=1))
            low.append(jnp.concatenate([pair[1] for pair in pairs], axis=1))
        rest = jnp.zeros((LANES - 2 * PY, S * LANES), BF16)
        right = jnp.concatenate(high[:per] + low[:per] + high[per:] + low[per:] + [rest], axis=0)
        sums = mxu(bands[c * 2 * GY : (c + 1) * 2 * GY, :], right)
        for s in range(S):
            total = None
            for n, turn in enumerate(groups):
                span, lanes = slice(n * Y, (n + 1) * Y), slice(s * LANES, (s + 1) * LANES)
                term = moved(sums[span, lanes] + sums[GY + n * Y : GY + (n + 1) * Y, lanes], turn)
                total = term if total is None else total + term
            cells = pl.ds((s * C + c) * Y, Y)
            res[cells, :] = dirty[cells, :] - total

    def gather_res(c, carry):
        for s in range(S):
            source = (s * C + c) * Y
            target = pl.ds(aligned((c * S + s) * Y), Y)
            slots[target, :] = permute(lambda y: jnp.broadcast_to(res[pl.ds(source + y, 1), :], (8, LANES)))
        return carry

    def halo_blocks(first, end, side, k, ok):
        blocks = recv_h.at[first:end, k]

        @pl.when(ok)
        def _():
            await_bytes(blocks, got_h.at[side, k])

        @pl.when(jnp.logical_not(ok))
        def _():
            blocks[...] = jnp.zeros(blocks.shape, F32)

    def send_slots(k):
        pack(send_r, k, slots)
        for copy in own_copies(lambda p: send_r.at[p, k], lambda p: recv_r.at[p, k], 3, got_r.at[k]):
            copy.start()
        recv_r[g, k] = send_r[g, k]

    for k in range(NCH):
        await_bytes(recv_m.at[0:last, k], got_m.at[k])
        halo_blocks(0, HALF // R, 1, k, has_next)
        halo_blocks(HALF // R, G, 0, k, has_prev)
        for q in range(G):
            from_next = q * R < HALF
            at_row = Y + HALF + q * R if from_next else q * R - HALF
            for r in range(R):
                padded[pl.ds(k * W * PY + HALF + q * R + r, W, stride=PY), :] = recv_m[
                    q, k, r * W : r * W + W, :
                ]
                padded[pl.ds(k * W * PY + at_row + r, W, stride=PY), :] = recv_h[
                    q, k, r * W : r * W + W, :
                ]
        for c in range(k * CC, (k + 1) * CC):
            convolve(c)
        for c in range(k * CC, (k + 1) * CC):
            gather_res(c, 0)
        send_slots(k)

    await_bytes(recv_d.at[0:last], got_d.at[0])
    project(recv_d)

    def shrink_slots(i, carry):
        top = pl.ds(pl.multiple_of(i * BLOCK, BLOCK), BLOCK)
        low = pl.ds(pl.multiple_of(DEPTHS + i * BLOCK, BLOCK), BLOCK)
        first_slots[top, :], first_slots[low, :] = shrink_pair(big[top, :], big[low, :])
        return carry

    lax.fori_loop(0, DEPTHS // BLOCK, shrink_slots, 0)

    for k in range(NCH):
        await_bytes(recv_r.at[0:last, k], got_r.at[k])
    project(recv_r)

    for kind, ref in enumerate((send_a, send_d, send_m, send_r)):
        await_bytes(ref.at[0:last], sent.at[kind])

    @pl.when(goes)
    def _():
        await_bytes(send_m, sent.at[4])


PARTS = 4


def finish_kernel(R, update, first, cells, out, res, stage, sems):
    copies = [pltpu.make_async_copy(cells, res, sems.at[0])]
    copies[0].start()
    block = 16

    def shrink_second(i, carry):
        top = pl.ds(pl.multiple_of(i * block, block), block)
        low = pl.ds(pl.multiple_of(DEPTHS + i * block, block), block)
        a, b = shrink_pair(
            first[top, :] + STEP_SIZE * update[top, :], first[low, :] + STEP_SIZE * update[low, :]
        )
        for start, value in ((0, a), (DEPTHS, b)):
            for r in range(R):
                stage[pl.ds((start + i * block) * R + r, block, stride=R), :] = value[
                    :, r * LANES : (r + 1) * LANES
                ]
        return carry

    steps = DEPTHS // block // PARTS
    rows = DEPTHS * R // PARTS
    for part in range(PARTS):
        lax.fori_loop(part * steps, (part + 1) * steps, shrink_second, 0)
        for half in range(2):
            span = pl.ds(half * DEPTHS * R + part * rows, rows)
            copy = pltpu.make_async_copy(stage.at[span], out.at[span], sems.at[1 + 2 * part + half])
            copy.start()
            copies.append(copy)
    for copy in copies:
        copy.wait()


def on_device(dirty, beams, chan_bins, pixel_order):
    S, C, Y, X = dirty.shape
    G = lax.axis_size("chan")
    T = lax.axis_size("tile")
    BEAM = math.isqrt(beams.shape[1])
    HALF = (BEAM - 1) // 2
    R = Y // G
    CC = 3 if C % 3 == 0 else C
    NCH = C // CC
    W = S * CC
    SC = S * C
    KP = round_up(G * SC, 16)
    K3 = round_up(3 * KP, LANES)
    PB = round_up(R * W, 8)
    N = R * X
    d = dict(G=G, T=T, R=R, Y=Y, C=C, S=S, W=W, CC=CC, NCH=NCH, HALF=HALF, BEAM=BEAM, KP=KP, K3=K3)
    vmem = pl.BlockSpec(memory_space=pltpu.VMEM)
    hbm = pl.BlockSpec(memory_space=pltpu.HBM)
    block = pltpu.VMEM((G, NCH, PB, LANES), F32)
    dma = pltpu.SemaphoreType.DMA
    args = (dirty.reshape(SC * Y, X), beams, chan_bins, pixel_order.reshape(Y, X))
    update, first, cells = pl.pallas_call(
        functools.partial(kernel, d),
        out_shape=(
            jax.ShapeDtypeStruct((2 * DEPTHS, N), F32),
            jax.ShapeDtypeStruct((2 * DEPTHS, N), F32),
            jax.ShapeDtypeStruct((SC * Y, X), F32),
        ),
        in_specs=[hbm, hbm, hbm, hbm],
        out_specs=(vmem, vmem, vmem),
        scratch_shapes=[
            pltpu.VMEM((SC * Y, X), F32),
            pltpu.VMEM(beams.shape, F32),
            pltpu.SMEM(chan_bins.shape, jnp.int32),
            pltpu.VMEM((Y, X), jnp.int32),
            pltpu.VMEM((pl.cdiv(beams.shape[1], LANES) * round_up(C, 8), LANES), F32),
            pltpu.VMEM((2 * len(hops(HALF)) * Y, LANES), jnp.int32),
            pltpu.VMEM((C * 2 * len(hops(HALF)) * Y, 3 * LANES), BF16),
            pltpu.VMEM((KP, LANES), F32),
            pltpu.VMEM((K3, 2 * DEPTHS), F32),
            pltpu.VMEM((2 * DEPTHS, K3), BF16),
            pltpu.VMEM((2 * KP, 2 * DEPTHS), BF16),
            pltpu.VMEM((KP, N), F32),
            pltpu.VMEM((2 * DEPTHS, N), BF16),
            pltpu.VMEM((2 * DEPTHS, N), BF16),
            pltpu.VMEM((KP, N), F32),
            pltpu.VMEM(((SC + 1) * (Y + 2 * HALF), LANES), F32),
            pltpu.VMEM(((SC + 1) * Y, LANES), F32),
            pltpu.VMEM(((SC + 1) * Y, LANES), F32),
        ]
        + [block] * 9
        + [dma((5,)), dma((1,)), dma((1,)), dma((NCH,)), dma((2, NCH)), dma((NCH,)), dma((4,))]
        + [pltpu.SemaphoreType.REGULAR],
        compiler_params=pltpu.CompilerParams(
            collective_id=0, has_side_effects=True, vmem_limit_bytes=40 * 1024 * 1024
        ),
    )(*(pltpu.with_memory_space_constraint(arg, pltpu.HBM) for arg in args))
    spectrum, residual = pl.pallas_call(
        functools.partial(finish_kernel, R),
        out_shape=(
            jax.ShapeDtypeStruct((2 * DEPTHS * R, LANES), F32),
            jax.ShapeDtypeStruct((SC * Y, X), F32),
        ),
        in_specs=[vmem, vmem, vmem],
        out_specs=(hbm, hbm),
        scratch_shapes=[pltpu.VMEM((2 * DEPTHS * R + 8, LANES), F32), dma((1 + 2 * PARTS,))],
        compiler_params=pltpu.CompilerParams(vmem_limit_bytes=8 * 1024 * 1024),
    )(update, first, cells)
    return spectrum.reshape(2, DEPTHS, 1, N), residual.reshape(dirty.shape)


def solution(mesh):
    placed = (P(None, "chan", "tile", None), P("chan", None), P(), P("tile", None))
    return jax.shard_map(
        on_device,
        mesh=mesh,
        in_specs=placed,
        out_specs=(P(None, None, "tile", "chan"), P(None, "chan", "tile", None)),
        check_vma=False,
    )
```

```python
import functools
import math

import jax
import jax.numpy as jnp
from jax import lax
from jax.experimental import pallas as pl
from jax.experimental.pallas import tpu as pltpu
from jax.sharding import PartitionSpec as P

DEPTHS = 256
BINS = 288
THRESHOLD = 0.8
STEP_SIZE = 0.5
MESH = pl.DeviceIdType.MESH
LANES = 128
REACH = 2
F32 = jnp.float32
BF16 = jnp.bfloat16


def round_up(value, unit):
    return (value + unit - 1) // unit * unit


def split(x):
    high = x.astype(BF16)
    return high, (x - high.astype(F32)).astype(BF16)


def shrink_pair(a, b):
    squared = a * a + b * b
    factor = jnp.maximum(1.0 - THRESHOLD * lax.rsqrt(jnp.maximum(squared, 1e-30)), 0.0)
    return a * factor, b * factor


def hops(half):
    last = -((REACH - half) // (REACH + 1))
    return [(REACH + 1) * m for m in range(-last, last + 1)]


def aligned(row):
    return row if isinstance(row, int) else pl.multiple_of(row, 8)


def mxu(a, b):
    return jnp.dot(a, b, preferred_element_type=F32)


def kernel(
    d,
    dirty_hbm,
    blocks_hbm,
    beams_hbm,
    bins_hbm,
    order_hbm,
    big,
    first_slots,
    res,
    dirty,
    beams,
    bins,
    order,
    wide,
    places,
    bands,
    bincol,
    at3,
    a3,
    at2,
    first_hi,
    first_lo,
    padded,
    slots_d,
    slots_r,
    send_m,
    recv_a,
    recv_d,
    recv_r,
    sent,
    got_a,
    got_d,
    got_m,
    got_h,
    got_r,
    sems_in,
    sems_own,
    joined,
):
    G, T, R, Y, C, S, CC, NCH, HALF, BEAM = (
        d["G"], d["T"], d["R"], d["Y"], d["C"], d["S"], d["CC"], d["NCH"], d["HALF"], d["BEAM"]
    )
    SC = S * C
    KP = d["KP"]
    X = LANES
    PY = Y + 2 * HALF
    g = lax.axis_index("chan")
    t = lax.axis_index("tile")
    has_prev = t > 0
    has_next = t < T - 1
    before = lax.rem(t + T - 1, T)
    after = lax.rem(t + 1, T)

    pairs = ((dirty_hbm, dirty), (bins_hbm, bins), (beams_hbm, beams), (order_hbm, order))
    loads = [pltpu.make_async_copy(src, dst, sems_in.at[n]) for n, (src, dst) in enumerate(pairs)]
    from_a, from_d, from_r = (ref.reshape(G, S, C, R, X) for ref in (recv_a, recv_d, recv_r))
    to_d, to_r = (ref.reshape(S, C, G, R, X) for ref in (slots_d, slots_r))
    to_m = send_m.reshape(G, S, C, R, X)
    rows = padded.reshape(S, C, PY // R, R, X)
    own_a = pltpu.make_async_copy(blocks_hbm.at[:, :, g], from_a.at[g], sems_own.at[0])
    for load in loads:
        load.start()
    own_a.start()
    last, lead = G - 1, G - 2
    barrier = pltpu.get_barrier_semaphore()
    for p in range(last):

        @pl.when(g != p)
        def _():
            pl.semaphore_signal(barrier, inc=1, device_id=(p, t), device_id_type=MESH)

    for edge, start in ((has_prev, 0), (has_next, Y + HALF)):

        @pl.when(jnp.logical_not(edge))
        def _():
            for image in range(SC):
                padded[image * PY + start : image * PY + start + HALF, :] = jnp.zeros((HALF, X), F32)

    @pl.when(g != last)
    def _():
        pl.semaphore_wait(barrier, G - 1)

    @pl.when(g == lead)
    def _():
        pl.semaphore_signal(joined, inc=1, device_id=(last, t), device_id_type=MESH)

        @pl.when(has_prev)
        def _():
            pl.semaphore_signal(barrier, inc=1, device_id=(last, before), device_id_type=MESH)

        @pl.when(has_next)
        def _():
            pl.semaphore_signal(barrier, inc=1, device_id=(last, after), device_id_type=MESH)

    @pl.when(g == last)
    def _():
        pl.semaphore_wait(joined, 1)

    def own_copies(src, dst, kind, got):
        copies = []
        for step in range(1, G):
            p = lax.rem(g + step, G)
            copies.append(
                pltpu.make_async_remote_copy(
                    src(p), dst(g), sent.at[kind], got, device_id=(p, t), device_id_type=MESH
                )
            )
        return copies

    def await_bytes(ref, sem):
        pltpu.make_async_copy(ref, ref, sem).wait()

    for copy in own_copies(lambda p: blocks_hbm.at[:, :, p], lambda p: from_a.at[p], 0, got_a.at[0]):
        copy.start()

    for load in loads:
        load.wait()
    shift = int(math.log2(LANES))

    def permute(cells):
        halves = []
        for h in range(Y // 8):
            pixel = order[8 * h : 8 * h + 8, :]
            col = pixel & (LANES - 1)
            row = lax.shift_right_logical(pixel, shift)
            acc = jnp.zeros((8, LANES), F32)
            for y in range(Y):
                taken = jnp.take_along_axis(cells(y), col, axis=1, mode="promise_in_bounds")
                acc = jnp.where(row == y, taken, acc)
            halves.append(acc)
        return jnp.concatenate(halves, axis=0)

    def gather_dirty(c, carry):
        for s in range(S):
            source = (s * C + c) * Y
            slots_d[pl.ds(aligned(source), Y), :] = permute(
                lambda y: jnp.broadcast_to(dirty[pl.ds(source + y, 1), :], (8, LANES))
            )
        return carry

    lax.fori_loop(0, C, gather_dirty, 0)
    for copy in own_copies(lambda p: to_d.at[:, :, p], lambda p: from_d.at[p], 1, got_d.at[0]):
        copy.start()
    own_d = pltpu.make_async_copy(to_d.at[:, :, g], from_d.at[g], sems_own.at[1])
    own_d.start()
    bincol[...] = jnp.zeros_like(bincol)
    for q in range(G):
        for c in range(C):
            for s in range(S):
                row = q * SC + s * C + c
                bincol[row : row + 1, :] = jnp.full((1, LANES), bins[q * C + c].astype(F32))
    scale = 1.0 / math.sqrt(G * C)
    at3[...] = jnp.zeros_like(at3)
    for piece in range(DEPTHS // LANES):
        shape = (KP, LANES)
        depth = lax.broadcasted_iota(jnp.int32, shape, 1) + (piece * LANES - DEPTHS // 2)
        product = bincol[...] * depth.astype(F32)
        turns = product - BINS * jnp.floor(product * (1.0 / BINS))
        turns = jnp.where(turns < 0, turns + BINS, turns)
        turns = jnp.where(turns >= BINS, turns - BINS, turns)
        angles = turns * (2.0 * math.pi / BINS)
        row = lax.broadcasted_iota(jnp.int32, shape, 0)
        is_q = lax.rem(row, SC) < C
        real = row < G * SC
        cosine = jnp.where(real, jnp.cos(angles) * scale, 0.0)
        sine = jnp.where(real, jnp.sin(angles) * scale, 0.0)
        for half, value in ((0, jnp.where(is_q, cosine, sine)), (1, jnp.where(is_q, -sine, cosine))):
            lanes = pl.ds(half * DEPTHS + piece * LANES, LANES)
            high, low = split(value)
            at2[0:KP, lanes] = high
            at2[KP : 2 * KP, lanes] = low
            at3[0:KP, lanes] = high.astype(F32)
            at3[KP : 2 * KP, lanes] = low.astype(F32)
            at3[2 * KP : 3 * KP, lanes] = high.astype(F32)
    turned = at3[...].T.astype(BF16)
    for n in range(DEPTHS // 16):
        for half in range(2):
            span = pl.ds((2 * n + half) * 16, 16)
            a3[span, :] = turned[half * DEPTHS + n * 16 : half * DEPTHS + n * 16 + 16, :]

    groups = hops(HALF)
    GY = len(groups) * Y
    near_lanes = list(range(-REACH, REACH + 1))
    per = LANES // PY
    wide[...] = jnp.zeros_like(wide)
    CP = round_up(C, 8)
    chunks = wide.shape[0] // CP
    for m in range(chunks):
        size = min(LANES, BEAM * BEAM - m * LANES)
        wide[m * CP : m * CP + C, 0:size] = beams[:, m * LANES : m * LANES + size]
    lane8 = lax.broadcasted_iota(jnp.int32, (8, LANES), 1)
    line8 = lax.broadcasted_iota(jnp.int32, (8, LANES), 0)
    for n, turn in enumerate(groups):
        low = -REACH if turn <= 0 else 0
        high = REACH if turn >= 0 else 0
        for y in range(0, Y, 8):
            i = lax.rem(lane8, PY) - (line8 + y)
            for block in range(2):
                j0 = lane8 // PY - REACH if block == 0 else jnp.where(lane8 < 2 * PY, REACH, LANES)
                j = j0 + (HALF + turn)
                ok = (i >= 0) & (i < BEAM) & (j0 >= low) & (j0 <= high) & (j >= 0) & (j < BEAM)
                places[pl.ds((block * len(groups) + n) * Y + y, 8), :] = jnp.where(ok, i * BEAM + j, -1)

    def band(c, carry):
        rows = [
            jnp.broadcast_to(wide[pl.ds(m * CP + c, 1), :], (8, LANES)) for m in range(chunks)
        ]
        for n, turn in enumerate(groups):
            parts = []
            for block in range(2):
                if block == 1 and turn < 0:
                    parts.append((jnp.zeros((Y, LANES), BF16),) * 2)
                    continue
                halves = []
                for y in range(0, Y, 8):
                    place = places[pl.ds((block * len(groups) + n) * Y + y, 8), :]
                    col = place & (LANES - 1)
                    row = lax.shift_right_arithmetic(place, shift)
                    acc = jnp.zeros((8, LANES), F32)
                    for m, source in enumerate(rows):
                        taken = jnp.take_along_axis(source, col, axis=1, mode="promise_in_bounds")
                        acc = jnp.where(row == m, taken, acc)
                    halves.append(acc)
                parts.append(split(jnp.concatenate(halves, axis=0)))
            for h in range(2):
                target = pl.ds(pl.multiple_of(c * (2 * GY) + h * GY + n * Y, 16), Y)
                bands[target, 0:LANES] = parts[0][h]
                bands[target, LANES : 2 * LANES] = parts[0][h]
                bands[target, 2 * LANES : 3 * LANES] = parts[1][h]
        return carry


    def project(recv):
        blank = jnp.zeros((KP - G * SC, LANES), F32)
        columns = [recv[pl.ds(r, G * SC, stride=R), :] for r in range(R)]
        if KP > G * SC:
            columns = [jnp.concatenate([column, blank], axis=0) for column in columns]
        high, low = split(jnp.concatenate(columns, axis=1))
        parts = [high, high, low]
        if d["K3"] > 3 * KP:
            parts.append(jnp.zeros((d["K3"] - 3 * KP, R * LANES), BF16))
        return mxu(a3[...], jnp.concatenate(parts, axis=0))

    def pairs_of(product):
        for n in range(DEPTHS // BLOCK):
            at = 2 * n * BLOCK
            yield n * BLOCK, product[at : at + BLOCK, :], product[at + BLOCK : at + 2 * BLOCK, :]

    BLOCK = 16

    @pl.when(g == last)
    def _():
        pl.semaphore_wait(barrier, has_prev.astype(jnp.int32) + has_next.astype(jnp.int32))
        for p in range(last):
            pl.semaphore_signal(joined, inc=1, device_id=(p, t), device_id_type=MESH)

    await_bytes(from_a.at[0:last], got_a.at[0])
    own_a.wait()
    for k, a, b in pairs_of(project(recv_a)):
        a, b = shrink_pair(a, b)
        first_hi[k : k + BLOCK, :], first_lo[k : k + BLOCK, :] = split(a)
        low = slice(DEPTHS + k, DEPTHS + k + BLOCK)
        first_hi[low, :], first_lo[low, :] = split(b)
    both = mxu(at2[...], first_hi[...])
    model = both[:KP] + both[KP:] + mxu(at2[0:KP, :], first_lo[...])
    for r in range(R):
        send_m[pl.ds(r, G * SC, stride=R), :] = model[: G * SC, r * LANES : (r + 1) * LANES]

    up = g * R < HALF
    goes = jnp.logical_or(jnp.logical_and(up, has_prev), jnp.logical_and(jnp.logical_not(up), has_next))
    toward = jnp.where(up, before, after)
    copies_h, own_m, own_r = [], [], []
    spot = jnp.where(up, (HALF + Y) // R + g, g - HALF // R)
    chunks_of = [slice(k * CC, (k + 1) * CC) for k in range(NCH)]

    @pl.when(g != last)
    def _():
        pl.semaphore_wait(joined, 1)

    for k in range(NCH):
        halo = [
            pltpu.make_async_remote_copy(
                to_m.at[p, :, chunks_of[k]],
                rows.at[:, chunks_of[k], spot],
                sent.at[4],
                got_h.at[up.astype(jnp.int32), k],
                device_id=(p, toward),
                device_id_type=MESH,
            )
            for p in range(G)
        ]
        copies_h.append(halo)

        @pl.when(goes)
        def _():
            for copy in halo:
                copy.start()

        for copy in own_copies(
            lambda p: to_m.at[p, :, chunks_of[k]],
            lambda p: rows.at[:, chunks_of[k], HALF // R + p],
            2,
            got_m.at[k],
        ):
            copy.start()
        own_m.append(
            pltpu.make_async_copy(
                to_m.at[g, :, chunks_of[k]], rows.at[:, chunks_of[k], HALF // R + g], sems_own.at[2 + k]
            )
        )
        own_m[k].start()

    lax.fori_loop(0, C, band, 0)

    lane = lax.broadcasted_iota(jnp.int32, (PY, LANES), 1)

    def moved(rows, by):
        if by == 0:
            return rows
        at = lane[: rows.shape[0]] + by
        return jnp.where((at >= 0) & (at < LANES), pltpu.roll(rows, (-by) % LANES, axis=1), 0.0)

    def convolve(c):
        images = [padded[pl.ds((s * C + c) * PY, PY), :] for s in range(S)]
        high, low = [], []
        for by in near_lanes:
            pairs = [split(moved(image, by)) for image in images]
            high.append(jnp.concatenate([pair[0] for pair in pairs], axis=1))
            low.append(jnp.concatenate([pair[1] for pair in pairs], axis=1))
        rest = jnp.zeros((LANES - 2 * PY, S * LANES), BF16)
        right = jnp.concatenate(high[:per] + low[:per] + high[per:] + low[per:] + [rest], axis=0)
        sums = mxu(bands[c * 2 * GY : (c + 1) * 2 * GY, :], right)
        for s in range(S):
            total = None
            for n, turn in enumerate(groups):
                span, lanes = slice(n * Y, (n + 1) * Y), slice(s * LANES, (s + 1) * LANES)
                term = moved(sums[span, lanes] + sums[GY + n * Y : GY + (n + 1) * Y, lanes], turn)
                total = term if total is None else total + term
            cells = pl.ds((s * C + c) * Y, Y)
            res[cells, :] = dirty[cells, :] - total

    def gather_res(c):
        for s in range(S):
            source = (s * C + c) * Y
            slots_r[pl.ds(source, Y), :] = permute(
                lambda y: jnp.broadcast_to(res[pl.ds(source + y, 1), :], (8, LANES))
            )

    def await_halo(side, k, ok):
        @pl.when(ok)
        def _():
            await_bytes(to_m.at[0 : HALF // R, :, chunks_of[k]], got_h.at[side, k])

    def send_slots(k):
        for copy in own_copies(
            lambda p: to_r.at[:, chunks_of[k], p], lambda p: from_r.at[p, :, chunks_of[k]], 3, got_r.at[k]
        ):
            copy.start()
        own_r.append(
            pltpu.make_async_copy(
                to_r.at[:, chunks_of[k], g], from_r.at[g, :, chunks_of[k]], sems_own.at[2 + NCH + k]
            )
        )
        own_r[k].start()

    for k in range(NCH):
        await_bytes(to_m.at[0:last, :, chunks_of[k]], got_m.at[k])
        own_m[k].wait()
        await_halo(1, k, has_next)
        await_halo(0, k, has_prev)
        for c in range(k * CC, (k + 1) * CC):
            convolve(c)
        for c in range(k * CC, (k + 1) * CC):
            gather_res(c)
        send_slots(k)

    await_bytes(from_d.at[0:last], got_d.at[0])
    own_d.wait()
    for k, a, b in pairs_of(project(recv_d)):
        first_slots[k : k + BLOCK, :], first_slots[DEPTHS + k : DEPTHS + k + BLOCK, :] = shrink_pair(a, b)

    for k in range(NCH):
        await_bytes(from_r.at[0:last, :, chunks_of[k]], got_r.at[k])
        own_r[k].wait()
    for k, a, b in pairs_of(project(recv_r)):
        big[k : k + BLOCK, :], big[DEPTHS + k : DEPTHS + k + BLOCK, :] = a, b

    for kind in range(4):
        await_bytes(from_a.at[0:last], sent.at[kind])

    @pl.when(goes)
    def _():
        await_bytes(from_a, sent.at[4])


PARTS = 4


def finish_kernel(R, update, first, cells, out, res, stage, sems):
    copies = [pltpu.make_async_copy(cells, res, sems.at[0])]
    copies[0].start()
    block = 16

    def shrink_second(i, carry):
        top = pl.ds(pl.multiple_of(i * block, block), block)
        low = pl.ds(pl.multiple_of(DEPTHS + i * block, block), block)
        a, b = shrink_pair(
            first[top, :] + STEP_SIZE * update[top, :], first[low, :] + STEP_SIZE * update[low, :]
        )
        for start, value in ((0, a), (DEPTHS, b)):
            for r in range(R):
                stage[pl.ds((start + i * block) * R + r, block, stride=R), :] = value[
                    :, r * LANES : (r + 1) * LANES
                ]
        return carry

    steps = DEPTHS // block // PARTS
    rows = DEPTHS * R // PARTS
    for part in range(PARTS):
        lax.fori_loop(part * steps, (part + 1) * steps, shrink_second, 0)
        for half in range(2):
            span = pl.ds(half * DEPTHS * R + part * rows, rows)
            copy = pltpu.make_async_copy(stage.at[span], out.at[span], sems.at[1 + 2 * part + half])
            copy.start()
            copies.append(copy)
    for copy in copies:
        copy.wait()


def on_device(dirty, beams, chan_bins, pixel_order):
    S, C, Y, X = dirty.shape
    G = lax.axis_size("chan")
    T = lax.axis_size("tile")
    BEAM = math.isqrt(beams.shape[1])
    HALF = (BEAM - 1) // 2
    R = Y // G
    CC = 3 if C % 3 == 0 else C
    NCH = C // CC
    SC = S * C
    KP = round_up(G * SC, 16)
    K3 = round_up(3 * KP, LANES)
    N = R * X
    d = dict(G=G, T=T, R=R, Y=Y, C=C, S=S, CC=CC, NCH=NCH, HALF=HALF, BEAM=BEAM, KP=KP, K3=K3)
    vmem = pl.BlockSpec(memory_space=pltpu.VMEM)
    hbm = pl.BlockSpec(memory_space=pltpu.HBM)
    share = pltpu.VMEM((G * SC * R, LANES), F32)
    strip = pltpu.VMEM((SC * Y, LANES), F32)
    dma = pltpu.SemaphoreType.DMA
    args = (dirty.reshape(SC * Y, X), dirty.reshape(S, C, G, R, X), beams, chan_bins, pixel_order.reshape(Y, X))
    update, first, cells = pl.pallas_call(
        functools.partial(kernel, d),
        out_shape=(
            jax.ShapeDtypeStruct((2 * DEPTHS, N), F32),
            jax.ShapeDtypeStruct((2 * DEPTHS, N), F32),
            jax.ShapeDtypeStruct((SC * Y, X), F32),
        ),
        in_specs=[hbm, hbm, hbm, hbm, hbm],
        out_specs=(vmem, vmem, vmem),
        scratch_shapes=[
            pltpu.VMEM((SC * Y, X), F32),
            pltpu.VMEM(beams.shape, F32),
            pltpu.SMEM(chan_bins.shape, jnp.int32),
            pltpu.VMEM((Y, X), jnp.int32),
            pltpu.VMEM((pl.cdiv(beams.shape[1], LANES) * round_up(C, 8), LANES), F32),
            pltpu.VMEM((2 * len(hops(HALF)) * Y, LANES), jnp.int32),
            pltpu.VMEM((C * 2 * len(hops(HALF)) * Y, 3 * LANES), BF16),
            pltpu.VMEM((KP, LANES), F32),
            pltpu.VMEM((K3, 2 * DEPTHS), F32),
            pltpu.VMEM((2 * DEPTHS, K3), BF16),
            pltpu.VMEM((2 * KP, 2 * DEPTHS), BF16),
            pltpu.VMEM((2 * DEPTHS, N), BF16),
            pltpu.VMEM((2 * DEPTHS, N), BF16),
            pltpu.VMEM((SC * (Y + 2 * HALF), LANES), F32),
            strip,
            strip,
        ]
        + [share] * 4
        + [dma((5,)), dma((1,)), dma((1,)), dma((NCH,)), dma((2, NCH)), dma((NCH,)), dma((4,)), dma((2 + 2 * NCH,))]
        + [pltpu.SemaphoreType.REGULAR],
        compiler_params=pltpu.CompilerParams(
            collective_id=0, has_side_effects=True, vmem_limit_bytes=40 * 1024 * 1024
        ),
    )(*(pltpu.with_memory_space_constraint(arg, pltpu.HBM) for arg in args))
    spectrum, residual = pl.pallas_call(
        functools.partial(finish_kernel, R),
        out_shape=(
            jax.ShapeDtypeStruct((2 * DEPTHS * R, LANES), F32),
            jax.ShapeDtypeStruct((SC * Y, X), F32),
        ),
        in_specs=[vmem, vmem, vmem],
        out_specs=(hbm, hbm),
        scratch_shapes=[pltpu.VMEM((2 * DEPTHS * R + 8, LANES), F32), dma((1 + 2 * PARTS,))],
        compiler_params=pltpu.CompilerParams(vmem_limit_bytes=8 * 1024 * 1024),
    )(update, first, cells)
    return spectrum.reshape(2, DEPTHS, 1, N), residual.reshape(dirty.shape)


def solution(mesh):
    placed = (P(None, "chan", "tile", None), P("chan", None), P(), P("tile", None))
    return jax.shard_map(
        on_device,
        mesh=mesh,
        in_specs=placed,
        out_specs=(P(None, None, "tile", "chan"), P(None, "chan", "tile", None)),
        check_vma=False,
    )
```

```python
import functools
import math

import jax
import jax.numpy as jnp
from jax import lax
from jax.experimental import pallas as pl
from jax.experimental.pallas import tpu as pltpu
from jax.sharding import PartitionSpec as P

DEPTHS = 256
BINS = 288
THRESHOLD = 0.8
STEP_SIZE = 0.5
MESH = pl.DeviceIdType.MESH
LANES = 128
REACH = 2
BLOCK = 16
F32 = jnp.float32
BF16 = jnp.bfloat16


def round_up(value, unit):
    return (value + unit - 1) // unit * unit


def split(x):
    high = x.astype(BF16)
    return high, (x - high.astype(F32)).astype(BF16)


def shrink_pair(a, b):
    squared = a * a + b * b
    factor = jnp.maximum(1.0 - THRESHOLD * lax.rsqrt(jnp.maximum(squared, 1e-30)), 0.0)
    return a * factor, b * factor


def hops(half):
    last = -((REACH - half) // (REACH + 1))
    return [(REACH + 1) * m for m in range(-last, last + 1)]


def aligned(row):
    return row if isinstance(row, int) else pl.multiple_of(row, 8)


def pairs_of(product):
    for n in range(DEPTHS // BLOCK):
        at = 2 * n * BLOCK
        yield n * BLOCK, product[at : at + BLOCK, :], product[at + BLOCK : at + 2 * BLOCK, :]


def mxu(a, b):
    return jnp.dot(a, b, preferred_element_type=F32)


def kernel(
    d,
    dirty_hbm,
    blocks_hbm,
    beams_hbm,
    bins_hbm,
    order_hbm,
    right,
    a3,
    first_slots,
    res,
    dirty,
    beams,
    bins,
    order,
    wide,
    places,
    bands,
    bincol,
    at3,
    at2,
    first_hi,
    first_lo,
    padded,
    slots_d,
    slots_r,
    send_m,
    recv_a,
    recv_d,
    recv_r,
    sent,
    got_a,
    got_d,
    got_m,
    got_h,
    got_r,
    sems_in,
    sems_own,
    joined,
):
    G, T, R, Y, C, S, CC, NCH, HALF, BEAM = (
        d["G"], d["T"], d["R"], d["Y"], d["C"], d["S"], d["CC"], d["NCH"], d["HALF"], d["BEAM"]
    )
    SC = S * C
    KP = d["KP"]
    X = LANES
    PY = Y + 2 * HALF
    g = lax.axis_index("chan")
    t = lax.axis_index("tile")
    has_prev = t > 0
    has_next = t < T - 1
    before = lax.rem(t + T - 1, T)
    after = lax.rem(t + 1, T)

    pairs = ((dirty_hbm, dirty), (bins_hbm, bins), (beams_hbm, beams), (order_hbm, order))
    loads = [pltpu.make_async_copy(src, dst, sems_in.at[n]) for n, (src, dst) in enumerate(pairs)]
    from_a, from_d, from_r = (ref.reshape(G, S, C, R, X) for ref in (recv_a, recv_d, recv_r))
    to_d, to_r = (ref.reshape(S, C, G, R, X) for ref in (slots_d, slots_r))
    to_m = send_m.reshape(G, S, C, R, X)
    rows = padded.reshape(S, C, PY // R, R, X)
    own_a = pltpu.make_async_copy(blocks_hbm.at[:, :, g], from_a.at[g], sems_own.at[0])
    for load in loads:
        load.start()
    own_a.start()
    last, lead = G - 1, G - 2
    barrier = pltpu.get_barrier_semaphore()
    for p in range(last):

        @pl.when(g != p)
        def _():
            pl.semaphore_signal(barrier, inc=1, device_id=(p, t), device_id_type=MESH)

    for edge, start in ((has_prev, 0), (has_next, Y + HALF)):

        @pl.when(jnp.logical_not(edge))
        def _():
            for image in range(SC):
                padded[image * PY + start : image * PY + start + HALF, :] = jnp.zeros((HALF, X), F32)

    @pl.when(g != last)
    def _():
        pl.semaphore_wait(barrier, G - 1)

    @pl.when(g == lead)
    def _():
        pl.semaphore_signal(joined, inc=1, device_id=(last, t), device_id_type=MESH)

        @pl.when(has_prev)
        def _():
            pl.semaphore_signal(barrier, inc=1, device_id=(last, before), device_id_type=MESH)

        @pl.when(has_next)
        def _():
            pl.semaphore_signal(barrier, inc=1, device_id=(last, after), device_id_type=MESH)

    @pl.when(g == last)
    def _():
        pl.semaphore_wait(joined, 1)

    def own_copies(src, dst, kind, got):
        copies = []
        for step in range(1, G):
            p = lax.rem(g + step, G)
            copies.append(
                pltpu.make_async_remote_copy(
                    src(p), dst(g), sent.at[kind], got, device_id=(p, t), device_id_type=MESH
                )
            )
        return copies

    def await_bytes(ref, sem):
        pltpu.make_async_copy(ref, ref, sem).wait()

    for copy in own_copies(lambda p: blocks_hbm.at[:, :, p], lambda p: from_a.at[p], 0, got_a.at[0]):
        copy.start()

    for load in loads:
        load.wait()
    shift = int(math.log2(LANES))

    def permute(cells):
        halves = []
        for h in range(Y // 8):
            pixel = order[8 * h : 8 * h + 8, :]
            col = pixel & (LANES - 1)
            row = lax.shift_right_logical(pixel, shift)
            acc = jnp.zeros((8, LANES), F32)
            for y in range(Y):
                taken = jnp.take_along_axis(cells(y), col, axis=1, mode="promise_in_bounds")
                acc = jnp.where(row == y, taken, acc)
            halves.append(acc)
        return jnp.concatenate(halves, axis=0)

    def gather_dirty(c, carry):
        for s in range(S):
            source = (s * C + c) * Y
            slots_d[pl.ds(aligned(source), Y), :] = permute(
                lambda y: jnp.broadcast_to(dirty[pl.ds(source + y, 1), :], (8, LANES))
            )
        return carry

    lax.fori_loop(0, C, gather_dirty, 0)
    for copy in own_copies(lambda p: to_d.at[:, :, p], lambda p: from_d.at[p], 1, got_d.at[0]):
        copy.start()
    own_d = pltpu.make_async_copy(to_d.at[:, :, g], from_d.at[g], sems_own.at[1])
    own_d.start()
    bincol[...] = jnp.zeros_like(bincol)
    for q in range(G):
        for c in range(C):
            for s in range(S):
                row = q * SC + s * C + c
                bincol[row : row + 1, :] = jnp.full((1, LANES), bins[q * C + c].astype(F32))
    scale = 1.0 / math.sqrt(G * C)
    at3[...] = jnp.zeros_like(at3)
    for piece in range(DEPTHS // LANES):
        shape = (KP, LANES)
        depth = lax.broadcasted_iota(jnp.int32, shape, 1) + (piece * LANES - DEPTHS // 2)
        product = bincol[...] * depth.astype(F32)
        turns = product - BINS * jnp.floor(product * (1.0 / BINS))
        turns = jnp.where(turns < 0, turns + BINS, turns)
        turns = jnp.where(turns >= BINS, turns - BINS, turns)
        angles = turns * (2.0 * math.pi / BINS)
        row = lax.broadcasted_iota(jnp.int32, shape, 0)
        is_q = lax.rem(row, SC) < C
        real = row < G * SC
        cosine = jnp.where(real, jnp.cos(angles) * scale, 0.0)
        sine = jnp.where(real, jnp.sin(angles) * scale, 0.0)
        for half, value in ((0, jnp.where(is_q, cosine, sine)), (1, jnp.where(is_q, -sine, cosine))):
            lanes = pl.ds(half * DEPTHS + piece * LANES, LANES)
            high, low = split(value)
            at2[0:KP, lanes] = high
            at2[KP : 2 * KP, lanes] = low
            at3[0:KP, lanes] = high.astype(F32)
            at3[KP : 2 * KP, lanes] = low.astype(F32)
            at3[2 * KP : 3 * KP, lanes] = high.astype(F32)
    turned = at3[...].T.astype(BF16)
    for n in range(DEPTHS // 16):
        for half in range(2):
            span = pl.ds((2 * n + half) * 16, 16)
            a3[span, :] = turned[half * DEPTHS + n * 16 : half * DEPTHS + n * 16 + 16, :]

    groups = hops(HALF)
    GY = len(groups) * Y
    near_lanes = list(range(-REACH, REACH + 1))
    per = LANES // PY
    wide[...] = jnp.zeros_like(wide)
    CP = round_up(C, 8)
    chunks = wide.shape[0] // CP
    for m in range(chunks):
        size = min(LANES, BEAM * BEAM - m * LANES)
        wide[m * CP : m * CP + C, 0:size] = beams[:, m * LANES : m * LANES + size]
    lane8 = lax.broadcasted_iota(jnp.int32, (8, LANES), 1)
    line8 = lax.broadcasted_iota(jnp.int32, (8, LANES), 0)
    for n, turn in enumerate(groups):
        low = -REACH if turn <= 0 else 0
        high = REACH if turn >= 0 else 0
        for y in range(0, Y, 8):
            i = lax.rem(lane8, PY) - (line8 + y)
            for block in range(2):
                j0 = lane8 // PY - REACH if block == 0 else jnp.where(lane8 < 2 * PY, REACH, LANES)
                j = j0 + (HALF + turn)
                ok = (i >= 0) & (i < BEAM) & (j0 >= low) & (j0 <= high) & (j >= 0) & (j < BEAM)
                places[pl.ds((block * len(groups) + n) * Y + y, 8), :] = jnp.where(ok, i * BEAM + j, -1)

    def band(c, carry):
        rows = [
            jnp.broadcast_to(wide[pl.ds(m * CP + c, 1), :], (8, LANES)) for m in range(chunks)
        ]
        for n, turn in enumerate(groups):
            parts = []
            for block in range(2):
                if block == 1 and turn < 0:
                    parts.append((jnp.zeros((Y, LANES), BF16),) * 2)
                    continue
                halves = []
                for y in range(0, Y, 8):
                    place = places[pl.ds((block * len(groups) + n) * Y + y, 8), :]
                    col = place & (LANES - 1)
                    row = lax.shift_right_arithmetic(place, shift)
                    acc = jnp.zeros((8, LANES), F32)
                    for m, source in enumerate(rows):
                        taken = jnp.take_along_axis(source, col, axis=1, mode="promise_in_bounds")
                        acc = jnp.where(row == m, taken, acc)
                    halves.append(acc)
                parts.append(split(jnp.concatenate(halves, axis=0)))
            for h in range(2):
                target = pl.ds(pl.multiple_of(c * (2 * GY) + h * GY + n * Y, 16), Y)
                bands[target, 0:LANES] = parts[0][h]
                bands[target, LANES : 2 * LANES] = parts[0][h]
                bands[target, 2 * LANES : 3 * LANES] = parts[1][h]
        return carry


    def stacked(recv):
        blank = jnp.zeros((KP - G * SC, LANES), F32)
        columns = [recv[pl.ds(r, G * SC, stride=R), :] for r in range(R)]
        if KP > G * SC:
            columns = [jnp.concatenate([column, blank], axis=0) for column in columns]
        high, low = split(jnp.concatenate(columns, axis=1))
        parts = [high, high, low]
        if d["K3"] > 3 * KP:
            parts.append(jnp.zeros((d["K3"] - 3 * KP, R * LANES), BF16))
        return jnp.concatenate(parts, axis=0)

    def project(recv):
        return mxu(a3[...], stacked(recv))

    @pl.when(g == last)
    def _():
        pl.semaphore_wait(barrier, has_prev.astype(jnp.int32) + has_next.astype(jnp.int32))
        for p in range(last):
            pl.semaphore_signal(joined, inc=1, device_id=(p, t), device_id_type=MESH)

    await_bytes(from_a.at[0:last], got_a.at[0])
    own_a.wait()
    for k, a, b in pairs_of(project(recv_a)):
        a, b = shrink_pair(a, b)
        first_hi[k : k + BLOCK, :], first_lo[k : k + BLOCK, :] = split(a)
        low = slice(DEPTHS + k, DEPTHS + k + BLOCK)
        first_hi[low, :], first_lo[low, :] = split(b)
    both = mxu(at2[...], first_hi[...])
    model = both[:KP] + both[KP:] + mxu(at2[0:KP, :], first_lo[...])
    for r in range(R):
        send_m[pl.ds(r, G * SC, stride=R), :] = model[: G * SC, r * LANES : (r + 1) * LANES]

    up = g * R < HALF
    goes = jnp.logical_or(jnp.logical_and(up, has_prev), jnp.logical_and(jnp.logical_not(up), has_next))
    toward = jnp.where(up, before, after)
    copies_h = []
    spot = jnp.where(up, (HALF + Y) // R + g, g - HALF // R)
    chunks_of = [slice(k * CC, (k + 1) * CC) for k in range(NCH)]

    @pl.when(g != last)
    def _():
        pl.semaphore_wait(joined, 1)

    for k in range(NCH):
        halo = [
            pltpu.make_async_remote_copy(
                to_m.at[p, :, chunks_of[k]],
                rows.at[:, chunks_of[k], spot],
                sent.at[4],
                got_h.at[up.astype(jnp.int32), k],
                device_id=(p, toward),
                device_id_type=MESH,
            )
            for p in range(G)
        ]
        copies_h.append(halo)

        @pl.when(goes)
        def _():
            for copy in halo:
                copy.start()

        for copy in own_copies(
            lambda p: to_m.at[p, :, chunks_of[k]],
            lambda p: rows.at[:, chunks_of[k], HALF // R + p],
            2,
            got_m.at[k],
        ):
            copy.start()
        pltpu.make_async_copy(
            to_m.at[g, :, chunks_of[k]], rows.at[:, chunks_of[k], HALF // R + g], sems_own.at[2 + k]
        ).start()

    lax.fori_loop(0, C, band, 0)

    lane = lax.broadcasted_iota(jnp.int32, (PY, LANES), 1)

    def moved(rows, by):
        if by == 0:
            return rows
        at = lane[: rows.shape[0]] + by
        return jnp.where((at >= 0) & (at < LANES), pltpu.roll(rows, (-by) % LANES, axis=1), 0.0)

    def convolve(c):
        images = [padded[pl.ds(aligned((s * C + c) * PY), PY), :] for s in range(S)]
        high, low = [], []
        for by in near_lanes:
            pairs = [split(moved(image, by)) for image in images]
            high.append(jnp.concatenate([pair[0] for pair in pairs], axis=1))
            low.append(jnp.concatenate([pair[1] for pair in pairs], axis=1))
        rest = jnp.zeros((LANES - 2 * PY, S * LANES), BF16)
        right = jnp.concatenate(high[:per] + low[:per] + high[per:] + low[per:] + [rest], axis=0)
        sums = mxu(bands[pl.ds(pl.multiple_of(c * (2 * GY), 16), 2 * GY), :], right)
        for s in range(S):
            total = None
            for n, turn in enumerate(groups):
                span, lanes = slice(n * Y, (n + 1) * Y), slice(s * LANES, (s + 1) * LANES)
                term = moved(sums[span, lanes] + sums[GY + n * Y : GY + (n + 1) * Y, lanes], turn)
                total = term if total is None else total + term
            cells = pl.ds(aligned((s * C + c) * Y), Y)
            res[cells, :] = dirty[cells, :] - total

    def gather_res(c):
        for s in range(S):
            source = (s * C + c) * Y
            slots_r[pl.ds(aligned(source), Y), :] = permute(
                lambda y: jnp.broadcast_to(res[pl.ds(source + y, 1), :], (8, LANES))
            )

    def await_halo(side, k, ok):
        @pl.when(ok)
        def _():
            await_bytes(to_m.at[0 : HALF // R, :, 0:CC], got_h.at[side, k])

    def chunk(k, carry):
        channels = pl.ds(k * CC, CC)
        await_bytes(to_m.at[0:last, :, 0:CC], got_m.at[k])
        await_bytes(to_m.at[0, :, 0:CC], sems_own.at[2 + k])
        await_halo(1, k, has_next)
        await_halo(0, k, has_prev)
        for c in range(CC):
            convolve(k * CC + c)
        for c in range(CC):
            gather_res(k * CC + c)
        for copy in own_copies(
            lambda p: to_r.at[:, channels, p], lambda p: from_r.at[p, :, channels], 3, got_r.at[k]
        ):
            copy.start()
        pltpu.make_async_copy(
            to_r.at[:, channels, g], from_r.at[g, :, channels], sems_own.at[2 + NCH + k]
        ).start()
        return carry

    lax.fori_loop(0, NCH, chunk, 0)

    await_bytes(from_d.at[0:last], got_d.at[0])
    own_d.wait()
    for k, a, b in pairs_of(project(recv_d)):
        first_slots[k : k + BLOCK, :], first_slots[DEPTHS + k : DEPTHS + k + BLOCK, :] = shrink_pair(a, b)

    for k in range(NCH):
        await_bytes(from_r.at[0:last, :, chunks_of[k]], got_r.at[k])
        await_bytes(from_r.at[0, :, chunks_of[k]], sems_own.at[2 + NCH + k])
    right[...] = stacked(recv_r)

    for kind in range(4):
        await_bytes(from_a.at[0:last], sent.at[kind])

    @pl.when(goes)
    def _():
        await_bytes(from_a, sent.at[4])


PARTS = 4


def finish_kernel(R, right, a3, first, cells, out, res, stage, sems):
    copies = [pltpu.make_async_copy(cells, res, sems.at[0])]
    copies[0].start()
    rows = DEPTHS * R // PARTS
    for k, a, b in pairs_of(mxu(a3[...], right[...])):
        low = DEPTHS + k
        pair = shrink_pair(
            first[k : k + BLOCK, :] + STEP_SIZE * a, first[low : low + BLOCK, :] + STEP_SIZE * b
        )
        for start, value in zip((k, low), pair):
            for r in range(R):
                stage[pl.ds(start * R + r, BLOCK, stride=R), :] = value[:, r * LANES : (r + 1) * LANES]
        part, rest = divmod(k + BLOCK, DEPTHS // PARTS)
        if rest == 0:
            for half in range(2):
                span = pl.ds(half * DEPTHS * R + (part - 1) * rows, rows)
                copy = pltpu.make_async_copy(stage.at[span], out.at[span], sems.at[2 * part - 1 + half])
                copy.start()
                copies.append(copy)
    for copy in copies:
        copy.wait()


def on_device(dirty, beams, chan_bins, pixel_order):
    S, C, Y, X = dirty.shape
    G = lax.axis_size("chan")
    T = lax.axis_size("tile")
    BEAM = math.isqrt(beams.shape[1])
    HALF = (BEAM - 1) // 2
    R = Y // G
    CC = 3 if C % 3 == 0 else C
    NCH = C // CC
    SC = S * C
    KP = round_up(G * SC, 16)
    K3 = round_up(3 * KP, LANES)
    N = R * X
    d = dict(G=G, T=T, R=R, Y=Y, C=C, S=S, CC=CC, NCH=NCH, HALF=HALF, BEAM=BEAM, KP=KP, K3=K3)
    vmem = pl.BlockSpec(memory_space=pltpu.VMEM)
    hbm = pl.BlockSpec(memory_space=pltpu.HBM)
    share = pltpu.VMEM((G * SC * R, LANES), F32)
    strip = pltpu.VMEM((SC * Y, LANES), F32)
    dma = pltpu.SemaphoreType.DMA
    args = (dirty.reshape(SC * Y, X), dirty.reshape(S, C, G, R, X), beams, chan_bins, pixel_order.reshape(Y, X))
    right, a3, first, cells = pl.pallas_call(
        functools.partial(kernel, d),
        out_shape=(
            jax.ShapeDtypeStruct((K3, N), BF16),
            jax.ShapeDtypeStruct((2 * DEPTHS, K3), BF16),
            jax.ShapeDtypeStruct((2 * DEPTHS, N), F32),
            jax.ShapeDtypeStruct((SC * Y, X), F32),
        ),
        in_specs=[hbm, hbm, hbm, hbm, hbm],
        out_specs=(vmem, vmem, vmem, vmem),
        scratch_shapes=[
            pltpu.VMEM((SC * Y, X), F32),
            pltpu.VMEM(beams.shape, F32),
            pltpu.SMEM(chan_bins.shape, jnp.int32),
            pltpu.VMEM((Y, X), jnp.int32),
            pltpu.VMEM((pl.cdiv(beams.shape[1], LANES) * round_up(C, 8), LANES), F32),
            pltpu.VMEM((2 * len(hops(HALF)) * Y, LANES), jnp.int32),
            pltpu.VMEM((C * 2 * len(hops(HALF)) * Y, 3 * LANES), BF16),
            pltpu.VMEM((KP, LANES), F32),
            pltpu.VMEM((K3, 2 * DEPTHS), F32),
            pltpu.VMEM((2 * KP, 2 * DEPTHS), BF16),
            pltpu.VMEM((2 * DEPTHS, N), BF16),
            pltpu.VMEM((2 * DEPTHS, N), BF16),
            pltpu.VMEM((SC * (Y + 2 * HALF), LANES), F32),
            strip,
            strip,
        ]
        + [share] * 4
        + [dma((5,)), dma((1,)), dma((1,)), dma((NCH,)), dma((2, NCH)), dma((NCH,)), dma((4,)), dma((2 + 2 * NCH,))]
        + [pltpu.SemaphoreType.REGULAR],
        compiler_params=pltpu.CompilerParams(
            collective_id=0, has_side_effects=True, vmem_limit_bytes=40 * 1024 * 1024
        ),
    )(*(pltpu.with_memory_space_constraint(arg, pltpu.HBM) for arg in args))
    spectrum, residual = pl.pallas_call(
        functools.partial(finish_kernel, R),
        out_shape=(
            jax.ShapeDtypeStruct((2 * DEPTHS * R, LANES), F32),
            jax.ShapeDtypeStruct((SC * Y, X), F32),
        ),
        in_specs=[vmem, vmem, vmem, vmem],
        out_specs=(hbm, hbm),
        scratch_shapes=[pltpu.VMEM((2 * DEPTHS * R + 8, LANES), F32), dma((1 + 2 * PARTS,))],
        compiler_params=pltpu.CompilerParams(vmem_limit_bytes=8 * 1024 * 1024),
    )(right, a3, first, cells)
    return spectrum.reshape(2, DEPTHS, 1, N), residual.reshape(dirty.shape)


def solution(mesh):
    placed = (P(None, "chan", "tile", None), P("chan", None), P(), P("tile", None))
    return jax.shard_map(
        on_device,
        mesh=mesh,
        in_specs=placed,
        out_specs=(P(None, None, "tile", "chan"), P(None, "chan", "tile", None)),
        check_vma=False,
    )
```

```python
import functools
import math

import jax
import jax.numpy as jnp
from jax import lax
from jax.experimental import pallas as pl
from jax.experimental.pallas import tpu as pltpu
from jax.sharding import PartitionSpec as P

DEPTHS = 256
BINS = 288
THRESHOLD = 0.8
STEP_SIZE = 0.5
MESH = pl.DeviceIdType.MESH
LANES = 128
REACH = 2
BLOCK = 16
F32 = jnp.float32
BF16 = jnp.bfloat16


def round_up(value, unit):
    return (value + unit - 1) // unit * unit


def split(x):
    high = x.astype(BF16)
    return high, (x - high.astype(F32)).astype(BF16)


def shrink_pair(a, b):
    squared = a * a + b * b
    factor = jnp.maximum(1.0 - THRESHOLD * lax.rsqrt(jnp.maximum(squared, 1e-30)), 0.0)
    return a * factor, b * factor


def hops(half):
    last = -((REACH - half) // (REACH + 1))
    return [(REACH + 1) * m for m in range(-last, last + 1)]


def aligned(row):
    return row if isinstance(row, int) else pl.multiple_of(row, 8)


def pairs_of(product):
    for n in range(DEPTHS // BLOCK):
        at = 2 * n * BLOCK
        yield n * BLOCK, product[at : at + BLOCK, :], product[at + BLOCK : at + 2 * BLOCK, :]


def mxu(a, b):
    return jnp.dot(a, b, preferred_element_type=F32)


def kernel(
    d,
    dirty_hbm,
    blocks_hbm,
    beams_hbm,
    bins_hbm,
    order_hbm,
    right,
    a3,
    first_slots,
    res,
    dirty,
    beams,
    bins,
    order,
    wide,
    places,
    bands,
    bincol,
    at3,
    at2,
    first_hi,
    first_lo,
    padded,
    slots_d,
    slots_r,
    send_m,
    recv_a,
    recv_d,
    recv_r,
    sent,
    got_a,
    got_d,
    got_m,
    got_h,
    got_r,
    sems_in,
    sems_own,
    joined,
):
    G, T, R, Y, C, S, CC, NCH, HALF, BEAM = (
        d["G"], d["T"], d["R"], d["Y"], d["C"], d["S"], d["CC"], d["NCH"], d["HALF"], d["BEAM"]
    )
    SC = S * C
    KP = d["KP"]
    X = LANES
    PY = Y + 2 * HALF
    g = lax.axis_index("chan")
    t = lax.axis_index("tile")
    has_prev = t > 0
    has_next = t < T - 1
    before = lax.rem(t + T - 1, T)
    after = lax.rem(t + 1, T)

    pairs = ((dirty_hbm, dirty), (bins_hbm, bins), (beams_hbm, beams), (order_hbm, order))
    loads = [pltpu.make_async_copy(src, dst, sems_in.at[n]) for n, (src, dst) in enumerate(pairs)]
    from_a, from_d, from_r = (ref.reshape(G, S, C, R, X) for ref in (recv_a, recv_d, recv_r))
    to_d, to_r = (ref.reshape(S, C, G, R, X) for ref in (slots_d, slots_r))
    to_m = send_m.reshape(G, S, C, R, X)
    rows = padded.reshape(S, C, PY // R, R, X)
    own_a = pltpu.make_async_copy(blocks_hbm.at[:, :, g], from_a.at[g], sems_own.at[0])
    for load in loads:
        load.start()
    own_a.start()
    last, lead = G - 1, G - 2
    barrier = pltpu.get_barrier_semaphore()
    for p in range(last):

        @pl.when(g != p)
        def _():
            pl.semaphore_signal(barrier, inc=1, device_id=(p, t), device_id_type=MESH)

    for edge, start in ((has_prev, 0), (has_next, Y + HALF)):

        @pl.when(jnp.logical_not(edge))
        def _():
            for image in range(SC):
                padded[image * PY + start : image * PY + start + HALF, :] = jnp.zeros((HALF, X), F32)

    @pl.when(g != last)
    def _():
        pl.semaphore_wait(barrier, G - 1)

    @pl.when(g == lead)
    def _():
        pl.semaphore_signal(joined, inc=1, device_id=(last, t), device_id_type=MESH)

        @pl.when(has_prev)
        def _():
            pl.semaphore_signal(barrier, inc=1, device_id=(last, before), device_id_type=MESH)

        @pl.when(has_next)
        def _():
            pl.semaphore_signal(barrier, inc=1, device_id=(last, after), device_id_type=MESH)

    @pl.when(g == last)
    def _():
        pl.semaphore_wait(joined, 1)

    def own_copies(src, dst, kind, got):
        copies = []
        for step in range(1, G):
            p = lax.rem(g + step, G)
            copies.append(
                pltpu.make_async_remote_copy(
                    src(p), dst(g), sent.at[kind], got, device_id=(p, t), device_id_type=MESH
                )
            )
        return copies

    def await_bytes(ref, sem):
        pltpu.make_async_copy(ref, ref, sem).wait()

    for copy in own_copies(lambda p: blocks_hbm.at[:, :, p], lambda p: from_a.at[p], 0, got_a.at[0]):
        copy.start()

    for load in loads:
        load.wait()
    shift = int(math.log2(LANES))

    def permute(cells):
        halves = []
        for h in range(Y // 8):
            pixel = order[8 * h : 8 * h + 8, :]
            col = pixel & (LANES - 1)
            row = lax.shift_right_logical(pixel, shift)
            acc = jnp.zeros((8, LANES), F32)
            for y in range(Y):
                taken = jnp.take_along_axis(cells(y), col, axis=1, mode="promise_in_bounds")
                acc = jnp.where(row == y, taken, acc)
            halves.append(acc)
        return jnp.concatenate(halves, axis=0)

    def gather_dirty(c, carry):
        for s in range(S):
            source = (s * C + c) * Y
            slots_d[pl.ds(aligned(source), Y), :] = permute(
                lambda y: jnp.broadcast_to(dirty[pl.ds(source + y, 1), :], (8, LANES))
            )
        return carry

    bincol[...] = jnp.zeros_like(bincol)
    for q in range(G):
        for c in range(C):
            for s in range(S):
                row = q * SC + s * C + c
                bincol[row : row + 1, :] = jnp.full((1, LANES), bins[q * C + c].astype(F32))
    scale = 1.0 / math.sqrt(G * C)
    at3[...] = jnp.zeros_like(at3)
    for piece in range(DEPTHS // LANES):
        shape = (KP, LANES)
        depth = lax.broadcasted_iota(jnp.int32, shape, 1) + (piece * LANES - DEPTHS // 2)
        product = bincol[...] * depth.astype(F32)
        turns = product - BINS * jnp.floor(product * (1.0 / BINS))
        turns = jnp.where(turns < 0, turns + BINS, turns)
        turns = jnp.where(turns >= BINS, turns - BINS, turns)
        angles = turns * (2.0 * math.pi / BINS)
        row = lax.broadcasted_iota(jnp.int32, shape, 0)
        is_q = lax.rem(row, SC) < C
        real = row < G * SC
        cosine = jnp.where(real, jnp.cos(angles) * scale, 0.0)
        sine = jnp.where(real, jnp.sin(angles) * scale, 0.0)
        for half, value in ((0, jnp.where(is_q, cosine, sine)), (1, jnp.where(is_q, -sine, cosine))):
            lanes = pl.ds(half * DEPTHS + piece * LANES, LANES)
            high, low = split(value)
            at2[0:KP, lanes] = high
            at2[KP : 2 * KP, lanes] = low
            at3[0:KP, lanes] = high.astype(F32)
            at3[KP : 2 * KP, lanes] = low.astype(F32)
            at3[2 * KP : 3 * KP, lanes] = high.astype(F32)
    turned = at3[...].T.astype(BF16)
    for n in range(DEPTHS // 16):
        for half in range(2):
            span = pl.ds((2 * n + half) * 16, 16)
            a3[span, :] = turned[half * DEPTHS + n * 16 : half * DEPTHS + n * 16 + 16, :]

    groups = hops(HALF)
    GY = len(groups) * Y
    near_lanes = list(range(-REACH, REACH + 1))
    per = LANES // PY
    wide[...] = jnp.zeros_like(wide)
    CP = round_up(C, 8)
    chunks = wide.shape[0] // CP
    for m in range(chunks):
        size = min(LANES, BEAM * BEAM - m * LANES)
        wide[m * CP : m * CP + C, 0:size] = beams[:, m * LANES : m * LANES + size]
    lane8 = lax.broadcasted_iota(jnp.int32, (8, LANES), 1)
    line8 = lax.broadcasted_iota(jnp.int32, (8, LANES), 0)
    for n, turn in enumerate(groups):
        low = -REACH if turn <= 0 else 0
        high = REACH if turn >= 0 else 0
        for y in range(0, Y, 8):
            i = lax.rem(lane8, PY) - (line8 + y)
            for block in range(2):
                j0 = lane8 // PY - REACH if block == 0 else jnp.where(lane8 < 2 * PY, REACH, LANES)
                j = j0 + (HALF + turn)
                ok = (i >= 0) & (i < BEAM) & (j0 >= low) & (j0 <= high) & (j >= 0) & (j < BEAM)
                places[pl.ds((block * len(groups) + n) * Y + y, 8), :] = jnp.where(ok, i * BEAM + j, -1)

    def band(c, carry):
        rows = [
            jnp.broadcast_to(wide[pl.ds(m * CP + c, 1), :], (8, LANES)) for m in range(chunks)
        ]
        for n, turn in enumerate(groups):
            parts = []
            for block in range(2):
                if block == 1 and turn < 0:
                    parts.append((jnp.zeros((Y, LANES), BF16),) * 2)
                    continue
                halves = []
                for y in range(0, Y, 8):
                    place = places[pl.ds((block * len(groups) + n) * Y + y, 8), :]
                    col = place & (LANES - 1)
                    row = lax.shift_right_arithmetic(place, shift)
                    acc = jnp.zeros((8, LANES), F32)
                    for m, source in enumerate(rows):
                        taken = jnp.take_along_axis(source, col, axis=1, mode="promise_in_bounds")
                        acc = jnp.where(row == m, taken, acc)
                    halves.append(acc)
                parts.append(split(jnp.concatenate(halves, axis=0)))
            for h in range(2):
                target = pl.ds(pl.multiple_of(c * (2 * GY) + h * GY + n * Y, 16), Y)
                bands[target, 0:LANES] = parts[0][h]
                bands[target, LANES : 2 * LANES] = parts[0][h]
                bands[target, 2 * LANES : 3 * LANES] = parts[1][h]
        return carry


    def stacked(recv):
        blank = jnp.zeros((KP - G * SC, LANES), F32)
        columns = [recv[pl.ds(r, G * SC, stride=R), :] for r in range(R)]
        if KP > G * SC:
            columns = [jnp.concatenate([column, blank], axis=0) for column in columns]
        high, low = split(jnp.concatenate(columns, axis=1))
        parts = [high, high, low]
        if d["K3"] > 3 * KP:
            parts.append(jnp.zeros((d["K3"] - 3 * KP, R * LANES), BF16))
        return jnp.concatenate(parts, axis=0)

    def project(recv):
        return mxu(a3[...], stacked(recv))

    @pl.when(g == last)
    def _():
        pl.semaphore_wait(barrier, has_prev.astype(jnp.int32) + has_next.astype(jnp.int32))
        for p in range(last):
            pl.semaphore_signal(joined, inc=1, device_id=(p, t), device_id_type=MESH)

    await_bytes(from_a.at[0:last], got_a.at[0])
    own_a.wait()
    for k, a, b in pairs_of(project(recv_a)):
        a, b = shrink_pair(a, b)
        first_hi[k : k + BLOCK, :], first_lo[k : k + BLOCK, :] = split(a)
        low = slice(DEPTHS + k, DEPTHS + k + BLOCK)
        first_hi[low, :], first_lo[low, :] = split(b)
    both = mxu(at2[...], first_hi[...])
    model = both[:KP] + both[KP:] + mxu(at2[0:KP, :], first_lo[...])
    for r in range(R):
        send_m[pl.ds(r, G * SC, stride=R), :] = model[: G * SC, r * LANES : (r + 1) * LANES]

    up = g * R < HALF
    goes = jnp.logical_or(jnp.logical_and(up, has_prev), jnp.logical_and(jnp.logical_not(up), has_next))
    toward = jnp.where(up, before, after)
    copies_h = []
    spot = jnp.where(up, (HALF + Y) // R + g, g - HALF // R)
    chunks_of = [slice(k * CC, (k + 1) * CC) for k in range(NCH)]

    @pl.when(g != last)
    def _():
        pl.semaphore_wait(joined, 1)

    for k in range(NCH):
        halo = [
            pltpu.make_async_remote_copy(
                to_m.at[p, :, chunks_of[k]],
                rows.at[:, chunks_of[k], spot],
                sent.at[4],
                got_h.at[up.astype(jnp.int32), k],
                device_id=(p, toward),
                device_id_type=MESH,
            )
            for p in range(G)
        ]
        copies_h.append(halo)

        @pl.when(goes)
        def _():
            for copy in halo:
                copy.start()

        for copy in own_copies(
            lambda p: to_m.at[p, :, chunks_of[k]],
            lambda p: rows.at[:, chunks_of[k], HALF // R + p],
            2,
            got_m.at[k],
        ):
            copy.start()
        pltpu.make_async_copy(
            to_m.at[g, :, chunks_of[k]], rows.at[:, chunks_of[k], HALF // R + g], sems_own.at[2 + k]
        ).start()

    lax.fori_loop(0, C, gather_dirty, 0)
    for copy in own_copies(lambda p: to_d.at[:, :, p], lambda p: from_d.at[p], 1, got_d.at[0]):
        copy.start()
    own_d = pltpu.make_async_copy(to_d.at[:, :, g], from_d.at[g], sems_own.at[1])
    own_d.start()
    lax.fori_loop(0, C, band, 0)

    lane = lax.broadcasted_iota(jnp.int32, (PY, LANES), 1)

    def moved(rows, by):
        if by == 0:
            return rows
        at = lane[: rows.shape[0]] + by
        return jnp.where((at >= 0) & (at < LANES), pltpu.roll(rows, (-by) % LANES, axis=1), 0.0)

    def convolve(c):
        images = [padded[pl.ds(aligned((s * C + c) * PY), PY), :] for s in range(S)]
        high, low = [], []
        for by in near_lanes:
            pairs = [split(moved(image, by)) for image in images]
            high.append(jnp.concatenate([pair[0] for pair in pairs], axis=1))
            low.append(jnp.concatenate([pair[1] for pair in pairs], axis=1))
        rest = jnp.zeros((LANES - 2 * PY, S * LANES), BF16)
        right = jnp.concatenate(high[:per] + low[:per] + high[per:] + low[per:] + [rest], axis=0)
        sums = mxu(bands[pl.ds(pl.multiple_of(c * (2 * GY), 16), 2 * GY), :], right)
        for s in range(S):
            total = None
            for n, turn in enumerate(groups):
                span, lanes = slice(n * Y, (n + 1) * Y), slice(s * LANES, (s + 1) * LANES)
                term = moved(sums[span, lanes] + sums[GY + n * Y : GY + (n + 1) * Y, lanes], turn)
                total = term if total is None else total + term
            cells = pl.ds(aligned((s * C + c) * Y), Y)
            res[cells, :] = dirty[cells, :] - total

    def gather_res(c):
        for s in range(S):
            source = (s * C + c) * Y
            slots_r[pl.ds(aligned(source), Y), :] = permute(
                lambda y: jnp.broadcast_to(res[pl.ds(source + y, 1), :], (8, LANES))
            )

    def await_halo(side, k, ok):
        @pl.when(ok)
        def _():
            await_bytes(to_m.at[0 : HALF // R, :, 0:CC], got_h.at[side, k])

    def chunk(k, carry):
        channels = pl.ds(k * CC, CC)
        await_bytes(to_m.at[0:last, :, 0:CC], got_m.at[k])
        await_bytes(to_m.at[0, :, 0:CC], sems_own.at[2 + k])
        await_halo(1, k, has_next)
        await_halo(0, k, has_prev)
        for c in range(CC):
            convolve(k * CC + c)
        for c in range(CC):
            gather_res(k * CC + c)
        for copy in own_copies(
            lambda p: to_r.at[:, channels, p], lambda p: from_r.at[p, :, channels], 3, got_r.at[k]
        ):
            copy.start()
        pltpu.make_async_copy(
            to_r.at[:, channels, g], from_r.at[g, :, channels], sems_own.at[2 + NCH + k]
        ).start()
        return carry

    lax.fori_loop(0, NCH, chunk, 0)

    await_bytes(from_d.at[0:last], got_d.at[0])
    own_d.wait()
    for k, a, b in pairs_of(project(recv_d)):
        first_slots[k : k + BLOCK, :], first_slots[DEPTHS + k : DEPTHS + k + BLOCK, :] = shrink_pair(a, b)

    for k in range(NCH):
        await_bytes(from_r.at[0:last, :, chunks_of[k]], got_r.at[k])
        await_bytes(from_r.at[0, :, chunks_of[k]], sems_own.at[2 + NCH + k])
    right[...] = stacked(recv_r)

    for kind in range(4):
        await_bytes(from_a.at[0:last], sent.at[kind])

    @pl.when(goes)
    def _():
        await_bytes(from_a, sent.at[4])


PARTS = 4


def finish_kernel(R, right, a3, first, cells, out, res, stage, sems):
    copies = [pltpu.make_async_copy(cells, res, sems.at[0])]
    copies[0].start()
    rows = DEPTHS * R // PARTS
    for k, a, b in pairs_of(mxu(a3[...], right[...])):
        low = DEPTHS + k
        pair = shrink_pair(
            first[k : k + BLOCK, :] + STEP_SIZE * a, first[low : low + BLOCK, :] + STEP_SIZE * b
        )
        for start, value in zip((k, low), pair):
            for r in range(R):
                stage[pl.ds(start * R + r, BLOCK, stride=R), :] = value[:, r * LANES : (r + 1) * LANES]
        part, rest = divmod(k + BLOCK, DEPTHS // PARTS)
        if rest == 0:
            for half in range(2):
                span = pl.ds(half * DEPTHS * R + (part - 1) * rows, rows)
                copy = pltpu.make_async_copy(stage.at[span], out.at[span], sems.at[2 * part - 1 + half])
                copy.start()
                copies.append(copy)
    for copy in copies:
        copy.wait()


def on_device(dirty, beams, chan_bins, pixel_order):
    S, C, Y, X = dirty.shape
    G = lax.axis_size("chan")
    T = lax.axis_size("tile")
    BEAM = math.isqrt(beams.shape[1])
    HALF = (BEAM - 1) // 2
    R = Y // G
    CC = 3 if C % 3 == 0 else C
    NCH = C // CC
    SC = S * C
    KP = round_up(G * SC, 16)
    K3 = round_up(3 * KP, LANES)
    N = R * X
    d = dict(G=G, T=T, R=R, Y=Y, C=C, S=S, CC=CC, NCH=NCH, HALF=HALF, BEAM=BEAM, KP=KP, K3=K3)
    vmem = pl.BlockSpec(memory_space=pltpu.VMEM)
    hbm = pl.BlockSpec(memory_space=pltpu.HBM)
    share = pltpu.VMEM((G * SC * R, LANES), F32)
    strip = pltpu.VMEM((SC * Y, LANES), F32)
    dma = pltpu.SemaphoreType.DMA
    args = (dirty.reshape(SC * Y, X), dirty.reshape(S, C, G, R, X), beams, chan_bins, pixel_order.reshape(Y, X))
    right, a3, first, cells = pl.pallas_call(
        functools.partial(kernel, d),
        out_shape=(
            jax.ShapeDtypeStruct((K3, N), BF16),
            jax.ShapeDtypeStruct((2 * DEPTHS, K3), BF16),
            jax.ShapeDtypeStruct((2 * DEPTHS, N), F32),
            jax.ShapeDtypeStruct((SC * Y, X), F32),
        ),
        in_specs=[hbm, hbm, hbm, hbm, hbm],
        out_specs=(vmem, vmem, vmem, vmem),
        scratch_shapes=[
            pltpu.VMEM((SC * Y, X), F32),
            pltpu.VMEM(beams.shape, F32),
            pltpu.SMEM(chan_bins.shape, jnp.int32),
            pltpu.VMEM((Y, X), jnp.int32),
            pltpu.VMEM((pl.cdiv(beams.shape[1], LANES) * round_up(C, 8), LANES), F32),
            pltpu.VMEM((2 * len(hops(HALF)) * Y, LANES), jnp.int32),
            pltpu.VMEM((C * 2 * len(hops(HALF)) * Y, 3 * LANES), BF16),
            pltpu.VMEM((KP, LANES), F32),
            pltpu.VMEM((K3, 2 * DEPTHS), F32),
            pltpu.VMEM((2 * KP, 2 * DEPTHS), BF16),
            pltpu.VMEM((2 * DEPTHS, N), BF16),
            pltpu.VMEM((2 * DEPTHS, N), BF16),
            pltpu.VMEM((SC * (Y + 2 * HALF), LANES), F32),
            strip,
            strip,
        ]
        + [share] * 4
        + [dma((5,)), dma((1,)), dma((1,)), dma((NCH,)), dma((2, NCH)), dma((NCH,)), dma((4,)), dma((2 + 2 * NCH,))]
        + [pltpu.SemaphoreType.REGULAR],
        compiler_params=pltpu.CompilerParams(
            collective_id=0, has_side_effects=True, vmem_limit_bytes=40 * 1024 * 1024
        ),
    )(*(pltpu.with_memory_space_constraint(arg, pltpu.HBM) for arg in args))
    spectrum, residual = pl.pallas_call(
        functools.partial(finish_kernel, R),
        out_shape=(
            jax.ShapeDtypeStruct((2 * DEPTHS * R, LANES), F32),
            jax.ShapeDtypeStruct((SC * Y, X), F32),
        ),
        in_specs=[vmem, vmem, vmem, vmem],
        out_specs=(hbm, hbm),
        scratch_shapes=[pltpu.VMEM((2 * DEPTHS * R + 8, LANES), F32), dma((1 + 2 * PARTS,))],
        compiler_params=pltpu.CompilerParams(vmem_limit_bytes=8 * 1024 * 1024),
    )(right, a3, first, cells)
    return spectrum.reshape(2, DEPTHS, 1, N), residual.reshape(dirty.shape)


def solution(mesh):
    placed = (P(None, "chan", "tile", None), P("chan", None), P(), P("tile", None))
    return jax.shard_map(
        on_device,
        mesh=mesh,
        in_specs=placed,
        out_specs=(P(None, None, "tile", "chan"), P(None, "chan", "tile", None)),
        check_vma=False,
    )
```

```python
import functools
import math

import jax
import jax.numpy as jnp
from jax import lax
from jax.experimental import pallas as pl
from jax.experimental.pallas import tpu as pltpu
from jax.sharding import PartitionSpec as P

DEPTHS = 256
BINS = 288
THRESHOLD = 0.8
STEP_SIZE = 0.5
MESH = pl.DeviceIdType.MESH
LANES = 128
REACH = 2
BLOCK = 16
F32 = jnp.float32
BF16 = jnp.bfloat16


def round_up(value, unit):
    return (value + unit - 1) // unit * unit


def split(x):
    high = x.astype(BF16)
    return high, (x - high.astype(F32)).astype(BF16)


def shrink_pair(a, b):
    squared = a * a + b * b
    factor = jnp.maximum(1.0 - THRESHOLD * lax.rsqrt(jnp.maximum(squared, 1e-30)), 0.0)
    return a * factor, b * factor


def hops(half):
    last = -((REACH - half) // (REACH + 1))
    return [(REACH + 1) * m for m in range(-last, last + 1)]


def aligned(row):
    return row if isinstance(row, int) else pl.multiple_of(row, 8)


def pairs_of(product):
    for n in range(DEPTHS // BLOCK):
        at = 2 * n * BLOCK
        yield n * BLOCK, product[at : at + BLOCK, :], product[at + BLOCK : at + 2 * BLOCK, :]


def mxu(a, b):
    return jnp.dot(a, b, preferred_element_type=F32)


def kernel(
    d,
    dirty_hbm,
    blocks_hbm,
    beams_hbm,
    bins_hbm,
    order_hbm,
    right,
    a3,
    first_slots,
    res,
    dirty,
    beams,
    bins,
    order,
    wide,
    places,
    bands,
    bincol,
    at3,
    at2,
    first_hi,
    first_lo,
    padded,
    slots_d,
    slots_r,
    send_m,
    recv_a,
    recv_d,
    recv_r,
    sent,
    got_a,
    got_d,
    got_m,
    got_h,
    got_r,
    sems_in,
    joined,
):
    G, T, R, Y, C, S, CC, NCH, HALF, BEAM = (
        d["G"], d["T"], d["R"], d["Y"], d["C"], d["S"], d["CC"], d["NCH"], d["HALF"], d["BEAM"]
    )
    SC = S * C
    KP = d["KP"]
    X = LANES
    PY = Y + 2 * HALF
    g = lax.axis_index("chan")
    t = lax.axis_index("tile")
    has_prev = t > 0
    has_next = t < T - 1
    before = lax.rem(t + T - 1, T)
    after = lax.rem(t + 1, T)

    pairs = ((dirty_hbm, dirty), (bins_hbm, bins), (beams_hbm, beams), (order_hbm, order))
    loads = [pltpu.make_async_copy(src, dst, sems_in.at[n]) for n, (src, dst) in enumerate(pairs)]
    from_a, from_d, from_r = (ref.reshape(G, S, C, R, X) for ref in (recv_a, recv_d, recv_r))
    to_d, to_r = (ref.reshape(S, C, G, R, X) for ref in (slots_d, slots_r))
    to_m = send_m.reshape(G, S, C, R, X)
    rows = padded.reshape(S, C, PY // R, R, X)
    own_a = pltpu.make_async_copy(blocks_hbm.at[:, :, g], from_a.at[g], got_a.at[0])
    for load in loads:
        load.start()
    own_a.start()
    last, lead = G - 1, G - 2
    barrier = pltpu.get_barrier_semaphore()
    for p in range(last):

        @pl.when(g != p)
        def _():
            pl.semaphore_signal(barrier, inc=1, device_id=(p, t), device_id_type=MESH)

    for edge, start in ((has_prev, 0), (has_next, Y + HALF)):

        @pl.when(jnp.logical_not(edge))
        def _():
            for image in range(SC):
                padded[image * PY + start : image * PY + start + HALF, :] = jnp.zeros((HALF, X), F32)

    @pl.when(g != last)
    def _():
        pl.semaphore_wait(barrier, G - 1)

    @pl.when(g == lead)
    def _():
        pl.semaphore_signal(joined, inc=1, device_id=(last, t), device_id_type=MESH)

        @pl.when(has_prev)
        def _():
            pl.semaphore_signal(barrier, inc=1, device_id=(last, before), device_id_type=MESH)

        @pl.when(has_next)
        def _():
            pl.semaphore_signal(barrier, inc=1, device_id=(last, after), device_id_type=MESH)

    @pl.when(g == last)
    def _():
        pl.semaphore_wait(joined, 1)

    def own_copies(src, dst, kind, got):
        copies = []
        for step in range(1, G):
            p = lax.rem(g + step, G)
            copies.append(
                pltpu.make_async_remote_copy(
                    src(p), dst(g), sent.at[kind], got, device_id=(p, t), device_id_type=MESH
                )
            )
        return copies

    def await_bytes(ref, sem):
        pltpu.make_async_copy(ref, ref, sem).wait()

    for copy in own_copies(lambda p: blocks_hbm.at[:, :, p], lambda p: from_a.at[p], 0, got_a.at[0]):
        copy.start()

    for load in loads:
        load.wait()
    shift = int(math.log2(LANES))

    def permute(cells):
        halves = []
        for h in range(Y // 8):
            pixel = order[8 * h : 8 * h + 8, :]
            col = pixel & (LANES - 1)
            row = lax.shift_right_logical(pixel, shift)
            acc = jnp.zeros((8, LANES), F32)
            for y in range(Y):
                taken = jnp.take_along_axis(cells(y), col, axis=1, mode="promise_in_bounds")
                acc = jnp.where(row == y, taken, acc)
            halves.append(acc)
        return jnp.concatenate(halves, axis=0)

    def gather_dirty(c, carry):
        for s in range(S):
            source = (s * C + c) * Y
            slots_d[pl.ds(aligned(source), Y), :] = permute(
                lambda y: jnp.broadcast_to(dirty[pl.ds(source + y, 1), :], (8, LANES))
            )
        return carry

    bincol[...] = jnp.zeros_like(bincol)
    for q in range(G):
        for c in range(C):
            for s in range(S):
                row = q * SC + s * C + c
                bincol[row : row + 1, :] = jnp.full((1, LANES), bins[q * C + c].astype(F32))
    scale = 1.0 / math.sqrt(G * C)
    at3[...] = jnp.zeros_like(at3)
    for piece in range(DEPTHS // LANES):
        shape = (KP, LANES)
        depth = lax.broadcasted_iota(jnp.int32, shape, 1) + (piece * LANES - DEPTHS // 2)
        product = bincol[...] * depth.astype(F32)
        turns = product - BINS * jnp.floor(product * (1.0 / BINS))
        turns = jnp.where(turns < 0, turns + BINS, turns)
        turns = jnp.where(turns >= BINS, turns - BINS, turns)
        angles = turns * (2.0 * math.pi / BINS)
        row = lax.broadcasted_iota(jnp.int32, shape, 0)
        is_q = lax.rem(row, SC) < C
        real = row < G * SC
        cosine = jnp.where(real, jnp.cos(angles) * scale, 0.0)
        sine = jnp.where(real, jnp.sin(angles) * scale, 0.0)
        for half, value in ((0, jnp.where(is_q, cosine, sine)), (1, jnp.where(is_q, -sine, cosine))):
            lanes = pl.ds(half * DEPTHS + piece * LANES, LANES)
            high, low = split(value)
            at2[0:KP, lanes] = high
            at2[KP : 2 * KP, lanes] = low
            at3[0:KP, lanes] = high.astype(F32)
            at3[KP : 2 * KP, lanes] = low.astype(F32)
            at3[2 * KP : 3 * KP, lanes] = high.astype(F32)
    turned = at3[...].T.astype(BF16)
    for n in range(DEPTHS // 16):
        for half in range(2):
            span = pl.ds((2 * n + half) * 16, 16)
            a3[span, :] = turned[half * DEPTHS + n * 16 : half * DEPTHS + n * 16 + 16, :]

    groups = hops(HALF)
    GY = len(groups) * Y
    near_lanes = list(range(-REACH, REACH + 1))
    per = LANES // PY
    wide[...] = jnp.zeros_like(wide)
    CP = round_up(C, 8)
    chunks = wide.shape[0] // CP
    for m in range(chunks):
        size = min(LANES, BEAM * BEAM - m * LANES)
        wide[m * CP : m * CP + C, 0:size] = beams[:, m * LANES : m * LANES + size]
    lane8 = lax.broadcasted_iota(jnp.int32, (8, LANES), 1)
    line8 = lax.broadcasted_iota(jnp.int32, (8, LANES), 0)
    for n, turn in enumerate(groups):
        low = -REACH if turn <= 0 else 0
        high = REACH if turn >= 0 else 0
        for y in range(0, Y, 8):
            i = lax.rem(lane8, PY) - (line8 + y)
            for block in range(2):
                j0 = lane8 // PY - REACH if block == 0 else jnp.where(lane8 < 2 * PY, REACH, LANES)
                j = j0 + (HALF + turn)
                ok = (i >= 0) & (i < BEAM) & (j0 >= low) & (j0 <= high) & (j >= 0) & (j < BEAM)
                places[pl.ds((block * len(groups) + n) * Y + y, 8), :] = jnp.where(ok, i * BEAM + j, -1)

    def band(c, carry):
        rows = [
            jnp.broadcast_to(wide[pl.ds(m * CP + c, 1), :], (8, LANES)) for m in range(chunks)
        ]
        for n, turn in enumerate(groups):
            parts = []
            for block in range(2):
                if block == 1 and turn < 0:
                    parts.append((jnp.zeros((Y, LANES), BF16),) * 2)
                    continue
                halves = []
                for y in range(0, Y, 8):
                    place = places[pl.ds((block * len(groups) + n) * Y + y, 8), :]
                    col = place & (LANES - 1)
                    row = lax.shift_right_arithmetic(place, shift)
                    acc = jnp.zeros((8, LANES), F32)
                    for m, source in enumerate(rows):
                        taken = jnp.take_along_axis(source, col, axis=1, mode="promise_in_bounds")
                        acc = jnp.where(row == m, taken, acc)
                    halves.append(acc)
                parts.append(split(jnp.concatenate(halves, axis=0)))
            for h in range(2):
                target = pl.ds(pl.multiple_of(c * (2 * GY) + h * GY + n * Y, 16), Y)
                bands[target, 0:LANES] = parts[0][h]
                bands[target, LANES : 2 * LANES] = parts[0][h]
                bands[target, 2 * LANES : 3 * LANES] = parts[1][h]
        return carry


    def stacked(recv):
        blank = jnp.zeros((KP - G * SC, LANES), F32)
        columns = [recv[pl.ds(r, G * SC, stride=R), :] for r in range(R)]
        if KP > G * SC:
            columns = [jnp.concatenate([column, blank], axis=0) for column in columns]
        high, low = split(jnp.concatenate(columns, axis=1))
        parts = [high, high, low]
        if d["K3"] > 3 * KP:
            parts.append(jnp.zeros((d["K3"] - 3 * KP, R * LANES), BF16))
        return jnp.concatenate(parts, axis=0)

    def project(recv):
        return mxu(a3[...], stacked(recv))

    @pl.when(g == last)
    def _():
        pl.semaphore_wait(barrier, has_prev.astype(jnp.int32) + has_next.astype(jnp.int32))
        for p in range(last):
            pl.semaphore_signal(joined, inc=1, device_id=(p, t), device_id_type=MESH)

    await_bytes(from_a, got_a.at[0])
    for k, a, b in pairs_of(project(recv_a)):
        a, b = shrink_pair(a, b)
        first_hi[k : k + BLOCK, :], first_lo[k : k + BLOCK, :] = split(a)
        low = slice(DEPTHS + k, DEPTHS + k + BLOCK)
        first_hi[low, :], first_lo[low, :] = split(b)
    both = mxu(at2[...], first_hi[...])
    model = both[:KP] + both[KP:] + mxu(at2[0:KP, :], first_lo[...])
    for r in range(R):
        send_m[pl.ds(r, G * SC, stride=R), :] = model[: G * SC, r * LANES : (r + 1) * LANES]

    up = g * R < HALF
    goes = jnp.logical_or(jnp.logical_and(up, has_prev), jnp.logical_and(jnp.logical_not(up), has_next))
    toward = jnp.where(up, before, after)
    copies_h = []
    spot = jnp.where(up, (HALF + Y) // R + g, g - HALF // R)
    chunks_of = [slice(k * CC, (k + 1) * CC) for k in range(NCH)]

    @pl.when(g != last)
    def _():
        pl.semaphore_wait(joined, 1)

    for k in range(NCH):
        halo = [
            pltpu.make_async_remote_copy(
                to_m.at[p, :, chunks_of[k]],
                rows.at[:, chunks_of[k], spot],
                sent.at[4],
                got_h.at[up.astype(jnp.int32), k],
                device_id=(p, toward),
                device_id_type=MESH,
            )
            for p in range(G)
        ]
        copies_h.append(halo)

        @pl.when(goes)
        def _():
            for copy in halo:
                copy.start()

        for copy in own_copies(
            lambda p: to_m.at[p, :, chunks_of[k]],
            lambda p: rows.at[:, chunks_of[k], HALF // R + p],
            2,
            got_m.at[k],
        ):
            copy.start()
        pltpu.make_async_copy(
            to_m.at[g, :, chunks_of[k]], rows.at[:, chunks_of[k], HALF // R + g], got_m.at[k]
        ).start()

    lax.fori_loop(0, C, gather_dirty, 0)
    for copy in own_copies(lambda p: to_d.at[:, :, p], lambda p: from_d.at[p], 1, got_d.at[0]):
        copy.start()
    pltpu.make_async_copy(to_d.at[:, :, g], from_d.at[g], got_d.at[0]).start()
    lax.fori_loop(0, C, band, 0)

    lane = lax.broadcasted_iota(jnp.int32, (PY, LANES), 1)

    def moved(rows, by):
        if by == 0:
            return rows
        at = lane[: rows.shape[0]] + by
        return jnp.where((at >= 0) & (at < LANES), pltpu.roll(rows, (-by) % LANES, axis=1), 0.0)

    def convolve(c):
        images = [padded[pl.ds(aligned((s * C + c) * PY), PY), :] for s in range(S)]
        high, low = [], []
        for by in near_lanes:
            pairs = [split(moved(image, by)) for image in images]
            high.append(jnp.concatenate([pair[0] for pair in pairs], axis=1))
            low.append(jnp.concatenate([pair[1] for pair in pairs], axis=1))
        rest = jnp.zeros((LANES - 2 * PY, S * LANES), BF16)
        right = jnp.concatenate(high[:per] + low[:per] + high[per:] + low[per:] + [rest], axis=0)
        sums = mxu(bands[pl.ds(pl.multiple_of(c * (2 * GY), 16), 2 * GY), :], right)
        for s in range(S):
            total = None
            for n, turn in enumerate(groups):
                span, lanes = slice(n * Y, (n + 1) * Y), slice(s * LANES, (s + 1) * LANES)
                term = moved(sums[span, lanes] + sums[GY + n * Y : GY + (n + 1) * Y, lanes], turn)
                total = term if total is None else total + term
            cells = pl.ds(aligned((s * C + c) * Y), Y)
            res[cells, :] = dirty[cells, :] - total

    def gather_res(c):
        for s in range(S):
            source = (s * C + c) * Y
            slots_r[pl.ds(aligned(source), Y), :] = permute(
                lambda y: jnp.broadcast_to(res[pl.ds(source + y, 1), :], (8, LANES))
            )

    def await_halo(side, k, ok):
        @pl.when(ok)
        def _():
            await_bytes(to_m.at[0 : HALF // R, :, 0:CC], got_h.at[side, k])

    def chunk(k, carry):
        channels = pl.ds(k * CC, CC)
        await_bytes(to_m.at[:, :, 0:CC], got_m.at[k])
        await_halo(1, k, has_next)
        await_halo(0, k, has_prev)
        for c in range(CC):
            convolve(k * CC + c)
        for c in range(CC):
            gather_res(k * CC + c)
        for copy in own_copies(
            lambda p: to_r.at[:, channels, p], lambda p: from_r.at[p, :, channels], 3, got_r.at[k]
        ):
            copy.start()
        pltpu.make_async_copy(
            to_r.at[:, channels, g], from_r.at[g, :, channels], got_r.at[k]
        ).start()
        return carry

    lax.fori_loop(0, NCH, chunk, 0)

    await_bytes(from_d, got_d.at[0])
    for k, a, b in pairs_of(project(recv_d)):
        first_slots[k : k + BLOCK, :], first_slots[DEPTHS + k : DEPTHS + k + BLOCK, :] = shrink_pair(a, b)

    for k in range(NCH):
        await_bytes(from_r.at[:, :, chunks_of[k]], got_r.at[k])
    right[...] = stacked(recv_r)

    for kind in range(4):
        await_bytes(from_a.at[0:last], sent.at[kind])

    @pl.when(goes)
    def _():
        await_bytes(from_a, sent.at[4])


PARTS = 4


def finish_kernel(R, right, a3, first, cells, out, res, stage, sems):
    copies = [pltpu.make_async_copy(cells, res, sems.at[0])]
    copies[0].start()
    rows = DEPTHS * R // PARTS
    for k, a, b in pairs_of(mxu(a3[...], right[...])):
        low = DEPTHS + k
        pair = shrink_pair(
            first[k : k + BLOCK, :] + STEP_SIZE * a, first[low : low + BLOCK, :] + STEP_SIZE * b
        )
        for start, value in zip((k, low), pair):
            for r in range(R):
                stage[pl.ds(start * R + r, BLOCK, stride=R), :] = value[:, r * LANES : (r + 1) * LANES]
        part, rest = divmod(k + BLOCK, DEPTHS // PARTS)
        if rest == 0:
            for half in range(2):
                span = pl.ds(half * DEPTHS * R + (part - 1) * rows, rows)
                copy = pltpu.make_async_copy(stage.at[span], out.at[span], sems.at[2 * part - 1 + half])
                copy.start()
                copies.append(copy)
    for copy in copies:
        copy.wait()


def on_device(dirty, beams, chan_bins, pixel_order):
    S, C, Y, X = dirty.shape
    G = lax.axis_size("chan")
    T = lax.axis_size("tile")
    BEAM = math.isqrt(beams.shape[1])
    HALF = (BEAM - 1) // 2
    R = Y // G
    CC = 3 if C % 3 == 0 else C
    NCH = C // CC
    SC = S * C
    KP = round_up(G * SC, 16)
    K3 = round_up(3 * KP, LANES)
    N = R * X
    d = dict(G=G, T=T, R=R, Y=Y, C=C, S=S, CC=CC, NCH=NCH, HALF=HALF, BEAM=BEAM, KP=KP, K3=K3)
    vmem = pl.BlockSpec(memory_space=pltpu.VMEM)
    hbm = pl.BlockSpec(memory_space=pltpu.HBM)
    share = pltpu.VMEM((G * SC * R, LANES), F32)
    strip = pltpu.VMEM((SC * Y, LANES), F32)
    dma = pltpu.SemaphoreType.DMA
    args = (dirty.reshape(SC * Y, X), dirty.reshape(S, C, G, R, X), beams, chan_bins, pixel_order.reshape(Y, X))
    right, a3, first, cells = pl.pallas_call(
        functools.partial(kernel, d),
        out_shape=(
            jax.ShapeDtypeStruct((K3, N), BF16),
            jax.ShapeDtypeStruct((2 * DEPTHS, K3), BF16),
            jax.ShapeDtypeStruct((2 * DEPTHS, N), F32),
            jax.ShapeDtypeStruct((SC * Y, X), F32),
        ),
        in_specs=[hbm, hbm, hbm, hbm, hbm],
        out_specs=(vmem, vmem, vmem, vmem),
        scratch_shapes=[
            pltpu.VMEM((SC * Y, X), F32),
            pltpu.VMEM(beams.shape, F32),
            pltpu.SMEM(chan_bins.shape, jnp.int32),
            pltpu.VMEM((Y, X), jnp.int32),
            pltpu.VMEM((pl.cdiv(beams.shape[1], LANES) * round_up(C, 8), LANES), F32),
            pltpu.VMEM((2 * len(hops(HALF)) * Y, LANES), jnp.int32),
            pltpu.VMEM((C * 2 * len(hops(HALF)) * Y, 3 * LANES), BF16),
            pltpu.VMEM((KP, LANES), F32),
            pltpu.VMEM((K3, 2 * DEPTHS), F32),
            pltpu.VMEM((2 * KP, 2 * DEPTHS), BF16),
            pltpu.VMEM((2 * DEPTHS, N), BF16),
            pltpu.VMEM((2 * DEPTHS, N), BF16),
            pltpu.VMEM((SC * (Y + 2 * HALF), LANES), F32),
            strip,
            strip,
        ]
        + [share] * 4
        + [dma((5,)), dma((1,)), dma((1,)), dma((NCH,)), dma((2, NCH)), dma((NCH,)), dma((4,))]
        + [pltpu.SemaphoreType.REGULAR],
        compiler_params=pltpu.CompilerParams(
            collective_id=0, has_side_effects=True, vmem_limit_bytes=40 * 1024 * 1024
        ),
    )(*(pltpu.with_memory_space_constraint(arg, pltpu.HBM) for arg in args))
    spectrum, residual = pl.pallas_call(
        functools.partial(finish_kernel, R),
        out_shape=(
            jax.ShapeDtypeStruct((2 * DEPTHS * R, LANES), F32),
            jax.ShapeDtypeStruct((SC * Y, X), F32),
        ),
        in_specs=[vmem, vmem, vmem, vmem],
        out_specs=(hbm, hbm),
        scratch_shapes=[pltpu.VMEM((2 * DEPTHS * R + 8, LANES), F32), dma((1 + 2 * PARTS,))],
        compiler_params=pltpu.CompilerParams(vmem_limit_bytes=8 * 1024 * 1024),
    )(right, a3, first, cells)
    return spectrum.reshape(2, DEPTHS, 1, N), residual.reshape(dirty.shape)


def solution(mesh):
    placed = (P(None, "chan", "tile", None), P("chan", None), P(), P("tile", None))
    return jax.shard_map(
        on_device,
        mesh=mesh,
        in_specs=placed,
        out_specs=(P(None, None, "tile", "chan"), P(None, "chan", "tile", None)),
        check_vma=False,
    )
```
